128 devices in a mesh: gx: 32 (over z, x, core), gy: 4 (over y).
Axes of the slice: x: 4, y: 4, z: 4, core: 2. Of those that a mesh axis runs over, the one named last changes fastest.
Arguments:
- forcing: float32 [6, 2, 4096, 512], P(None, None, 'gx', 'gy'), may hold values from -3 to 3
- gap_cubed: float32 [4096, 512], P('gx', 'gy'), may hold values from 0.5 to 2
- hole_mask: int32 [4096, 512], P('gx', 'gy'), may hold values 0 or 1
- coarse_bases: float32 [40, 4096, 512], P(None, 'gx', 'gy'), may hold values from -12 to 12
- basis_counts: int32 [32, 4], P('gx', 'gy'), may hold values from 8 to 40, as said below
Outputs:
- solution: float32 [6, 2, 4096, 512], P(None, None, 'gx', 'gy')
The draws below stay inside these ranges and needn't reach their ends.
Inputs may be any that keep to these rules, and one draw needn't show every extreme that they name: `basis_counts`: each tile uses the first of its 40 stored bases, at least 8 of them; some tile uses all 40 and some tile exactly 8.
All inputs are finite; a program needn't handle non-finite values. No bound on the sum of `hole_mask` on one device may be relied on, other than what follows from the above.
Results may differ from the reference program's by a relative error of at most 0.0003.
Values sent between devices are 32-bit elements; how exact they have to be, the bound alone decides.
A program may use at most 128 MiB of HBM per device.

```python
import math
import jax
import jax.numpy as jnp
from jax import lax

CX = 128
CY = 128
NRHS = 6
KMAX = 40
MARGIN = 16
SWEEPS = 20
CSTEPS = 7
ITERS = 2
TX = 32
TY = 4
NX = 4096
NY = 512


def draw_forcing(key, part):
    keys = jax.random.split(key, 4)
    x_cells = (jnp.arange(NX, dtype=jnp.float32) + 0.5) / NX
    y_cells = (jnp.arange(NY, dtype=jnp.float32) + 0.5) / NY
    wave_x = jax.random.randint(keys[0], (NRHS, 1, 1, 1), 1, 5).astype(jnp.float32)
    wave_y = jax.random.randint(keys[1], (NRHS, 1, 1, 1), 1, 4).astype(jnp.float32)
    phases = jax.random.uniform(keys[2], (NRHS, 2, 1, 1), jnp.float32, -math.pi, math.pi)
    smooth = jnp.cos(2.0 * math.pi * wave_x * x_cells[:, None] + phases) * jnp.sin(math.pi * wave_y * y_cells[None, :])
    rough = jnp.clip(0.5 * jax.random.normal(keys[3], (NRHS, 2, NX, NY), jnp.float32), -1.5, 1.5)
    return smooth + rough


def draw_coarse_bases(key, part):
    keys = jax.random.split(key, 3)
    noise = jnp.clip(jax.random.normal(keys[0], (KMAX, TX, CX, TY, CY), jnp.float32), -4.0, 4.0)
    scales = jnp.exp(jax.random.uniform(keys[1], (KMAX, TX, 1, TY, 1), jnp.float32, 0.0, math.log(10.0)))
    offsets = jax.random.uniform(keys[2], (KMAX, TX, 1, TY, 1), jnp.float32, 0.5, 1.5)
    values = scales * (noise + offsets) / math.sqrt(CX * CY)
    return values.reshape(KMAX, NX, NY)


def draw_basis_counts(key, part):
    keys = jax.random.split(key, 2)
    tiles = TX * TY
    flat = jax.random.randint(keys[0], (tiles,), 8, KMAX + 1)
    where_full = jax.random.randint(keys[1], (), 0, tiles)
    flat = flat.at[where_full].set(KMAX)
    flat = flat.at[(where_full + 1) % tiles].set(8)
    return flat.reshape(TX, TY)


def with_ends(entries, own_key, least, top_value):
    longest = entries.shape.index(max(entries.shape))
    spots = []
    for shift in (0, 1):
        where = [jax.random.randint(jax.random.fold_in(own_key, axis), (), 0, length) for axis, length in enumerate(entries.shape)]
        where[longest] = (where[longest] + shift) % entries.shape[longest]
        spots.append(tuple(where))
    return entries.at[spots[0]].set(least).at[spots[1]].set(top_value)


def block_levels(rng, dims, shards, least, high):
    def one(dim, parts):
        draws = jax.random.uniform(jax.random.fold_in(jax.random.fold_in(rng, 6), dim), (parts,), jnp.float32, least / len(shards), high / len(shards))
        return jnp.repeat(jnp.exp(draws), dims[dim] // parts).reshape((-1,) + (1,) * (len(dims) - dim - 1))

    level = one(*shards[0])
    for cut in shards[1:]:
        level = level * one(*cut)
    return level


def setup_inputs(seed: int = 0) -> dict:
    key_list = jax.random.split(jax.random.key(seed), 6)
    return {
        "forcing": draw_forcing(jax.random.fold_in(key_list[5], 71), 0),
        "gap_cubed": jnp.clip(jnp.exp(math.log(2.0) - 1.3862944 * jax.random.uniform(key_list[1], (NX, NY), jnp.float32) ** block_levels(key_list[1], (NX, NY), ((0, 32), (1, 4)), -0.2, 0.2)), 0.5, 2.0),
        "hole_mask": with_ends((jax.random.randint(key_list[2], (NX, NY), 0, 32) < 1).astype(jnp.int32), jax.random.fold_in(key_list[2], 1), 0, 1),
        "coarse_bases": draw_coarse_bases(jax.random.fold_in(key_list[5], 71), 0),
        "basis_counts": draw_basis_counts(jax.random.fold_in(key_list[5], 71), 0),
    }


squeeze_number = 0.2
vent_gain = 4.0
relaxation = 0.8
guard_value = 1e-12
highest = lax.Precision.HIGHEST


def edge_terms(gap_padded):
    centre = gap_padded[1:-1, 1:-1]
    north_edge = 0.5 * (centre + gap_padded[2:, 1:-1])
    south_edge = 0.5 * (centre + gap_padded[:-2, 1:-1])
    east_edge = 0.5 * (centre + gap_padded[1:-1, 2:])
    west_edge = 0.5 * (centre + gap_padded[1:-1, :-2])
    return north_edge, south_edge, east_edge, west_edge


def diagonal_of(edge_set, vent_term):
    return edge_set[0] + edge_set[1] + edge_set[2] + edge_set[3] + vent_term


def apply_operator(padded, edge_set, diagonal):
    north_edge, south_edge, east_edge, west_edge = edge_set
    centre = padded[:, :, 1:-1, 1:-1]
    beside_all = (north_edge * padded[:, :, 2:, 1:-1] + south_edge * padded[:, :, :-2, 1:-1]
              + east_edge * padded[:, :, 1:-1, 2:] + west_edge * padded[:, :, 1:-1, :-2])
    turned = jnp.stack([-centre[:, 1], centre[:, 0]], axis=1)
    return diagonal * centre - beside_all + squeeze_number * turned


def local_solve(residual, edge_set, diagonal, inside):
    real_diag = jnp.where(inside > 0, diagonal, 1.0)
    step_scale = relaxation * inside / (real_diag * real_diag + squeeze_number * squeeze_number)

    def sweep(sweep_index, iterate):
        padded = jnp.pad(iterate, ((0, 0), (0, 0), (1, 1), (1, 1)))
        defect = residual - apply_operator(padded, edge_set, diagonal)
        update_real = real_diag * defect[:, 0] + squeeze_number * defect[:, 1]
        update_imag = real_diag * defect[:, 1] - squeeze_number * defect[:, 0]
        return iterate + step_scale * jnp.stack([update_real, update_imag], axis=1)

    return lax.fori_loop(0, SWEEPS, sweep, jnp.zeros_like(residual))


def complex_scale(alpha_real, alpha_imag, vectors):
    return jnp.stack([alpha_real * vectors[..., 0] - alpha_imag * vectors[..., 1],
                      alpha_real * vectors[..., 1] + alpha_imag * vectors[..., 0]], axis=-1)


def pad_plate(array, width):
    wrapped = jnp.concatenate([array[..., -width:, :], array, array[..., :width, :]], axis=-2)
    widths = [(0, 0)] * (array.ndim - 1) + [(width, width)]
    return jnp.pad(wrapped, widths)


def reference(forcing, gap_cubed, hole_mask, coarse_bases, basis_counts):
    vent_term = vent_gain * hole_mask.astype(jnp.float32) * gap_cubed
    owned_edges = edge_terms(pad_plate(gap_cubed, 1))
    owned_diag = diagonal_of(owned_edges, vent_term)
    deep_width = MARGIN + 1
    gap_deep = pad_plate(gap_cubed, deep_width)
    vent_wide = pad_plate(vent_term, MARGIN)
    ext_rows = CX + 2 * MARGIN
    ext_cols = CY + 2 * MARGIN
    active = (jnp.arange(KMAX, dtype=jnp.int32)[:, None, None] < basis_counts[None]).astype(jnp.float32)
    tiled = coarse_bases.reshape(KMAX, TX, CX, TY, CY) * active[:, :, None, :, None]

    def restrict(pressure):
        blocks = pressure.reshape(NRHS, 2, TX, CX, TY, CY)
        return jnp.einsum("axiyj,ncxiyj->xyanc", tiled, blocks, precision=highest)

    def prolong(coarse):
        return jnp.einsum("axiyj,xyanc->ncxiyj", tiled, coarse, precision=highest).reshape(NRHS, 2, NX, NY)

    def operator(pressure):
        return apply_operator(pad_plate(pressure, 1), owned_edges, owned_diag)

    solution = jnp.zeros_like(forcing)
    for outer_step in range(ITERS):
        residual = forcing - operator(solution)
        residual_wide = pad_plate(residual, MARGIN)

        def solve_tile(tile_index):
            tile_x = tile_index // TY
            tile_y = tile_index % TY
            row_start = (tile_x * CX).astype(jnp.int32)
            col_start = (tile_y * CY).astype(jnp.int32)
            anchor = jnp.zeros((), jnp.int32)
            local_resid = lax.dynamic_slice(residual_wide, (anchor, anchor, row_start, col_start),
                                            (NRHS, 2, ext_rows, ext_cols))
            gap_local = lax.dynamic_slice(gap_deep, (row_start, col_start), (ext_rows + 2, ext_cols + 2))
            vent_local = lax.dynamic_slice(vent_wide, (row_start, col_start), (ext_rows, ext_cols))
            col_ids = col_start - MARGIN + jnp.arange(ext_cols, dtype=jnp.int32)
            inside = jnp.broadcast_to(((col_ids >= 0) & (col_ids < NY)).astype(jnp.float32)[None, :],
                                      (ext_rows, ext_cols))
            edge_set = edge_terms(gap_local)
            diagonal = diagonal_of(edge_set, vent_local)
            result = local_solve(local_resid, edge_set, diagonal, inside)
            return result[:, :, MARGIN:MARGIN + CX, MARGIN:MARGIN + CY]

        pieces = lax.map(solve_tile, jnp.arange(TX * TY, dtype=jnp.int32))
        local_part = pieces.reshape(TX, TY, NRHS, 2, CX, CY).transpose(2, 3, 0, 4, 1, 5).reshape(NRHS, 2, NX, NY)
        search = restrict(residual)
        coarse = jnp.zeros_like(search)
        for coarse_step in range(CSTEPS):
            images = restrict(operator(prolong(search)))
            num_real = jnp.sum(images[..., 0] * search[..., 0] + images[..., 1] * search[..., 1], axis=(0, 1, 2))
            num_imag = jnp.sum(images[..., 0] * search[..., 1] - images[..., 1] * search[..., 0], axis=(0, 1, 2))
            denominator = jnp.sum(images * images, axis=(0, 1, 2, 4)) + guard_value
            alpha_real = num_real / denominator
            alpha_imag = num_imag / denominator
            coarse = coarse + complex_scale(alpha_real, alpha_imag, search)
            search = search - complex_scale(alpha_real, alpha_imag, images)
        solution = solution + local_part + prolong(coarse)
    return solution
```

```python
import jax
import jax.numpy as jnp
from jax import lax
from jax.sharding import PartitionSpec as P

MARGIN = 16
SWEEPS = 20
CSTEPS = 7
ITERS = 2


squeeze_number = 0.2
vent_gain = 4.0
relaxation = 0.8
guard_value = 1e-12
highest = lax.Precision.HIGHEST


def padded_2(cells, sides, width):
    for axis, dim in sides:
        count = lax.axis_size(axis)
        head = lax.slice_in_dim(cells, 0, width, axis=dim)
        tail = lax.slice_in_dim(cells, cells.shape[dim] - width, cells.shape[dim], axis=dim)
        cells = jnp.concatenate(
            [
                lax.ppermute(tail, axis, [(i, (i + 1) % count) for i in range(count)]),
                cells,
                lax.ppermute(head, axis, [((i + 1) % count, i) for i in range(count)]),
            ],
            axis=dim,
        )
    return cells


def tree_sum(values, axes):
    for axis in axes:
        count = lax.axis_size(axis)
        if count & (count - 1):
            values = lax.psum(values, axis)
            continue
        stride = 1
        while stride < count:
            values = values + lax.ppermute(values, axis, [(i, i ^ stride) for i in range(count)])
            stride *= 2
    return values


def edge_terms(gap_padded):
    centre = gap_padded[1:-1, 1:-1]
    north_edge = 0.5 * (centre + gap_padded[2:, 1:-1])
    south_edge = 0.5 * (centre + gap_padded[:-2, 1:-1])
    east_edge = 0.5 * (centre + gap_padded[1:-1, 2:])
    west_edge = 0.5 * (centre + gap_padded[1:-1, :-2])
    return (north_edge, south_edge, east_edge, west_edge)


def diagonal_of(edge_set, vent_term):
    return edge_set[0] + edge_set[1] + edge_set[2] + edge_set[3] + vent_term


def apply_operator(padded, edge_set, diagonal):
    north_edge, south_edge, east_edge, west_edge = edge_set
    centre = padded[:, :, 1:-1, 1:-1]
    beside_all = (
        north_edge * padded[:, :, 2:, 1:-1]
        + south_edge * padded[:, :, :-2, 1:-1]
        + east_edge * padded[:, :, 1:-1, 2:]
        + west_edge * padded[:, :, 1:-1, :-2]
    )
    turned = jnp.stack([-centre[:, 1], centre[:, 0]], axis=1)
    return diagonal * centre - beside_all + squeeze_number * turned


def local_solve(residual, edge_set, diagonal, inside):
    real_diag = jnp.where(inside > 0, diagonal, 1.0)
    step_scale = relaxation * inside / (real_diag * real_diag + squeeze_number * squeeze_number)

    def sweep(sweep_index, iterate):
        padded = jnp.pad(iterate, ((0, 0), (0, 0), (1, 1), (1, 1)))
        defect = residual - apply_operator(padded, edge_set, diagonal)
        update_real = real_diag * defect[:, 0] + squeeze_number * defect[:, 1]
        update_imag = real_diag * defect[:, 1] - squeeze_number * defect[:, 0]
        return iterate + step_scale * jnp.stack([update_real, update_imag], axis=1)

    return lax.fori_loop(0, SWEEPS, sweep, jnp.zeros_like(residual))


def complex_scale(alpha_real, alpha_imag, vectors):
    return jnp.stack(
        [
            alpha_real * vectors[..., 0] - alpha_imag * vectors[..., 1],
            alpha_real * vectors[..., 1] + alpha_imag * vectors[..., 0],
        ],
        axis=-1,
    )


def plate_columns(width, tile_cols):
    first_col = lax.axis_index("gy") * tile_cols - width
    col_ids = first_col + jnp.arange(tile_cols + 2 * width, dtype=jnp.int32)
    return ((col_ids >= 0) & (col_ids < tile_cols * lax.axis_size("gy"))).astype(jnp.float32)


def body(forcing, gap_cubed, hole_mask, coarse_bases, basis_counts):
    mode_count = forcing.shape[0]
    tile_rows, tile_cols = gap_cubed.shape
    basis_total = coarse_bases.shape[0]
    deep_width = MARGIN + 1
    wide_rows = tile_rows + 2 * MARGIN
    wide_cols = tile_cols + 2 * MARGIN
    vent_term = vent_gain * hole_mask.astype(jnp.float32) * gap_cubed
    start_stack = jnp.concatenate(
        [gap_cubed[None], vent_term[None], forcing.reshape(2 * mode_count, tile_rows, tile_cols)],
        axis=0,
    )
    grown_stack = padded_2(start_stack, (("gx", 1), ("gy", 2)), deep_width)
    grown_stack = grown_stack * plate_columns(deep_width, tile_cols)
    gap_deep = grown_stack[0]
    vent_wide = grown_stack[1, 1:-1, 1:-1]
    force_wide = grown_stack[2:, 1:-1, 1:-1].reshape(mode_count, 2, wide_rows, wide_cols)
    inside = jnp.broadcast_to(plate_columns(MARGIN, tile_cols)[None, :], (wide_rows, wide_cols))
    wide_edges = edge_terms(gap_deep)
    wide_diag = diagonal_of(wide_edges, vent_wide)
    owned_edges = edge_terms(gap_deep[MARGIN:-MARGIN, MARGIN:-MARGIN])
    owned_diag = diagonal_of(owned_edges, vent_term)
    unit_mask = plate_columns(1, tile_cols)
    active = (jnp.arange(basis_total, dtype=jnp.int32) < basis_counts[0, 0]).astype(jnp.float32)
    base_field = coarse_bases * active[:, None, None]
    flat_bases = base_field.reshape(basis_total, tile_rows * tile_cols)

    def restrict(pressure):
        flat_field = pressure.reshape(2 * mode_count, tile_rows * tile_cols)
        product = lax.dot_general(
            flat_bases,
            flat_field,
            (((1,), (1,)), ((), ())),
            precision=highest,
            preferred_element_type=jnp.float32,
        )
        return product.reshape(basis_total, mode_count, 2)

    def prolong(coarse):
        product = lax.dot_general(
            coarse.reshape(basis_total, 2 * mode_count),
            flat_bases,
            (((0,), (0,)), ((), ())),
            precision=highest,
            preferred_element_type=jnp.float32,
        )
        return product.reshape(mode_count, 2, tile_rows, tile_cols)

    solution = jnp.zeros_like(forcing)
    residual_wide = force_wide
    for outer_step in range(ITERS):
        if outer_step > 0:
            padded = padded_2(solution, (("gx", 2), ("gy", 3)), 1) * unit_mask
            owned_resid = forcing - apply_operator(padded, owned_edges, owned_diag)
            residual_wide = padded_2(owned_resid, (("gx", 2), ("gy", 3)), MARGIN)
            residual_wide = residual_wide * plate_columns(MARGIN, tile_cols)
        residual = residual_wide[:, :, MARGIN:-MARGIN, MARGIN:-MARGIN]
        local_part = local_solve(residual_wide, wide_edges, wide_diag, inside)[
            :, :, MARGIN:-MARGIN, MARGIN:-MARGIN
        ]
        search = restrict(residual)
        coarse = jnp.zeros_like(search)
        for coarse_step in range(CSTEPS):
            coarse_padded = padded_2(prolong(search), (("gx", 2), ("gy", 3)), 1) * unit_mask
            images = restrict(apply_operator(coarse_padded, owned_edges, owned_diag))
            num_real = jnp.sum(
                images[..., 0] * search[..., 0] + images[..., 1] * search[..., 1], axis=0
            )
            num_imag = jnp.sum(
                images[..., 0] * search[..., 1] - images[..., 1] * search[..., 0], axis=0
            )
            squares = jnp.sum(images * images, axis=(0, 2))
            packed = tree_sum(jnp.concatenate([num_real, num_imag, squares]), ("gy", "gx"))
            num_real, num_imag, squares = jnp.split(packed, 3)
            denominator = squares + guard_value
            alpha_real = num_real / denominator
            alpha_imag = num_imag / denominator
            coarse = coarse + complex_scale(alpha_real, alpha_imag, search)
            search = search - complex_scale(alpha_real, alpha_imag, images)
        solution = solution + local_part + prolong(coarse)
    return solution


def solution(mesh):
    placed = (
        P(None, None, "gx", "gy"),
        P("gx", "gy"),
        P("gx", "gy"),
        P(None, "gx", "gy"),
        P("gx", "gy"),
    )
    return jax.shard_map(
        body, mesh=mesh, in_specs=placed, out_specs=P(None, None, "gx", "gy"), check_vma=False
    )
```

```python
import jax
import jax.numpy as jnp
from jax import lax
from jax.sharding import PartitionSpec as P

MARGIN = 16
SWEEPS = 20
CSTEPS = 7
ITERS = 2


squeeze_number = 0.2
vent_gain = 4.0
relaxation = 0.8
guard_value = 1e-12
highest = lax.Precision.HIGHEST


def padded_2(cells, sides, width):
    for axis, dim in sides:
        count = lax.axis_size(axis)
        head = lax.slice_in_dim(cells, 0, width, axis=dim)
        tail = lax.slice_in_dim(cells, cells.shape[dim] - width, cells.shape[dim], axis=dim)
        cells = jnp.concatenate(
            [
                lax.ppermute(tail, axis, [(i, (i + 1) % count) for i in range(count)]),
                cells,
                lax.ppermute(head, axis, [((i + 1) % count, i) for i in range(count)]),
            ],
            axis=dim,
        )
    return cells


def tree_sum(values, axes):
    for axis in axes:
        count = lax.axis_size(axis)
        if count & (count - 1):
            values = lax.psum(values, axis)
            continue
        stride = 1
        while stride < count:
            values = values + lax.ppermute(values, axis, [(i, i ^ stride) for i in range(count)])
            stride *= 2
    return values


def edge_terms(gap_padded):
    centre = gap_padded[1:-1, 1:-1]
    north_edge = 0.5 * (centre + gap_padded[2:, 1:-1])
    south_edge = 0.5 * (centre + gap_padded[:-2, 1:-1])
    east_edge = 0.5 * (centre + gap_padded[1:-1, 2:])
    west_edge = 0.5 * (centre + gap_padded[1:-1, :-2])
    return (north_edge, south_edge, east_edge, west_edge)


def diagonal_of(edge_set, vent_term):
    return edge_set[0] + edge_set[1] + edge_set[2] + edge_set[3] + vent_term


def apply_operator(padded, edge_set, diagonal):
    north_edge, south_edge, east_edge, west_edge = edge_set
    centre = padded[:, :, 1:-1, 1:-1]
    beside_all = (
        north_edge * padded[:, :, 2:, 1:-1]
        + south_edge * padded[:, :, :-2, 1:-1]
        + east_edge * padded[:, :, 1:-1, 2:]
        + west_edge * padded[:, :, 1:-1, :-2]
    )
    turned = jnp.stack([-centre[:, 1], centre[:, 0]], axis=1)
    return diagonal * centre - beside_all + squeeze_number * turned


def local_solve(residual, edge_set, diagonal, inside):
    real_diag = jnp.where(inside > 0, diagonal, 1.0)
    step_scale = relaxation * inside / (real_diag * real_diag + squeeze_number * squeeze_number)

    def sweep(sweep_index, iterate):
        padded = jnp.pad(iterate, ((0, 0), (0, 0), (1, 1), (1, 1)))
        defect = residual - apply_operator(padded, edge_set, diagonal)
        update_real = real_diag * defect[:, 0] + squeeze_number * defect[:, 1]
        update_imag = real_diag * defect[:, 1] - squeeze_number * defect[:, 0]
        return iterate + step_scale * jnp.stack([update_real, update_imag], axis=1)

    return lax.fori_loop(0, SWEEPS, sweep, jnp.zeros_like(residual))


def complex_scale(alpha_real, alpha_imag, vectors):
    return jnp.stack(
        [
            alpha_real * vectors[..., 0] - alpha_imag * vectors[..., 1],
            alpha_real * vectors[..., 1] + alpha_imag * vectors[..., 0],
        ],
        axis=-1,
    )


def plate_columns(width, tile_cols):
    first_col = lax.axis_index("gy") * tile_cols - width
    col_ids = first_col + jnp.arange(tile_cols + 2 * width, dtype=jnp.int32)
    return ((col_ids >= 0) & (col_ids < tile_cols * lax.axis_size("gy"))).astype(jnp.float32)


def body(forcing, gap_cubed, hole_mask, coarse_bases, basis_counts):
    mode_count = forcing.shape[0]
    tile_rows, tile_cols = gap_cubed.shape
    basis_total = coarse_bases.shape[0]
    deep_width = MARGIN + 1
    wide_rows = tile_rows + 2 * MARGIN
    wide_cols = tile_cols + 2 * MARGIN
    vent_term = vent_gain * hole_mask.astype(jnp.float32) * gap_cubed
    start_stack = jnp.concatenate(
        [gap_cubed[None], vent_term[None], forcing.reshape(2 * mode_count, tile_rows, tile_cols)],
        axis=0,
    )
    grown_stack = padded_2(start_stack, (("gx", 1), ("gy", 2)), deep_width)
    grown_stack = grown_stack * plate_columns(deep_width, tile_cols)
    gap_deep = grown_stack[0]
    vent_wide = grown_stack[1, 1:-1, 1:-1]
    force_wide = grown_stack[2:, 1:-1, 1:-1].reshape(mode_count, 2, wide_rows, wide_cols)
    inside = jnp.broadcast_to(plate_columns(MARGIN, tile_cols)[None, :], (wide_rows, wide_cols))
    wide_edges = edge_terms(gap_deep)
    wide_diag = diagonal_of(wide_edges, vent_wide)
    owned_edges = edge_terms(gap_deep[MARGIN:-MARGIN, MARGIN:-MARGIN])
    owned_diag = diagonal_of(owned_edges, vent_term)
    unit_mask = plate_columns(1, tile_cols)
    active = (jnp.arange(basis_total, dtype=jnp.int32) < basis_counts[0, 0]).astype(jnp.float32)
    base_field = coarse_bases * active[:, None, None]
    flat_bases = base_field.reshape(basis_total, tile_rows * tile_cols)

    def restrict(pressure):
        flat_field = pressure.reshape(2 * mode_count, tile_rows * tile_cols)
        product = lax.dot_general(
            flat_bases,
            flat_field,
            (((1,), (1,)), ((), ())),
            precision=highest,
            preferred_element_type=jnp.float32,
        )
        return product.reshape(basis_total, mode_count, 2)

    def prolong(coarse):
        product = lax.dot_general(
            coarse.reshape(basis_total, 2 * mode_count),
            flat_bases,
            (((0,), (0,)), ((), ())),
            precision=highest,
            preferred_element_type=jnp.float32,
        )
        return product.reshape(mode_count, 2, tile_rows, tile_cols)

    def pair(left, right):
        return lax.dot_general(
            left, right, (((1,), (1,)), ((), ())), precision=highest, preferred_element_type=jnp.float32
        )

    gx_count = lax.axis_size("gx")
    gy_count = lax.axis_size("gy")
    gy_index = lax.axis_index("gy")
    north_edge, south_edge, east_edge, west_edge = owned_edges
    from_next_x = lax.ppermute(base_field[:, 0, :], "gx", [((i + 1) % gx_count, i) for i in range(gx_count)])
    from_prev_x = lax.ppermute(base_field[:, -1, :], "gx", [(i, (i + 1) % gx_count) for i in range(gx_count)])
    from_next_y = lax.ppermute(base_field[:, :, 0], "gy", [((i + 1) % gy_count, i) for i in range(gy_count)])
    from_prev_y = lax.ppermute(base_field[:, :, -1], "gy", [(i, (i + 1) % gy_count) for i in range(gy_count)])
    has_next_y = (gy_index < gy_count - 1).astype(jnp.float32)
    has_prev_y = (gy_index > 0).astype(jnp.float32)
    base_padded = jnp.pad(base_field, ((0, 0), (1, 1), (1, 1)))
    base_image = owned_diag * base_field - (
        north_edge * base_padded[:, 2:, 1:-1]
        + south_edge * base_padded[:, :-2, 1:-1]
        + east_edge * base_padded[:, 1:-1, 2:]
        + west_edge * base_padded[:, 1:-1, :-2]
    )
    self_block = pair(flat_bases, base_image.reshape(basis_total, tile_rows * tile_cols))
    gram_block = pair(flat_bases, flat_bases)
    next_x_block = -pair(base_field[:, -1, :] * north_edge[-1], from_next_x)
    prev_x_block = -pair(base_field[:, 0, :] * south_edge[0], from_prev_x)
    next_y_block = -pair(base_field[:, :, -1] * east_edge[:, -1], from_next_y) * has_next_y
    prev_y_block = -pair(base_field[:, :, 0] * west_edge[:, 0], from_prev_y) * has_prev_y
    block_row = jnp.concatenate(
        [self_block, next_x_block, prev_x_block, next_y_block, prev_y_block, squeeze_number * gram_block],
        axis=1,
    )
    all_blocks = lax.all_gather(block_row, ("gx", "gy")).reshape(gx_count, gy_count, basis_total, 6 * basis_total)

    def coarse_image(search):
        turned = jnp.stack([-search[..., 1], search[..., 0]], axis=-1)
        stacked = jnp.concatenate(
            [
                search,
                jnp.roll(search, -1, axis=0),
                jnp.roll(search, 1, axis=0),
                jnp.roll(search, -1, axis=1),
                jnp.roll(search, 1, axis=1),
                turned,
            ],
            axis=2,
        )
        product = lax.dot_general(
            all_blocks,
            stacked.reshape(gx_count, gy_count, 6 * basis_total, 2 * mode_count),
            (((3,), (2,)), ((0, 1), (0, 1))),
            precision=highest,
            preferred_element_type=jnp.float32,
        )
        return product.reshape(search.shape)

    gx_index = lax.axis_index("gx")
    solution = jnp.zeros_like(forcing)
    residual_wide = force_wide
    for outer_step in range(ITERS):
        if outer_step > 0:
            padded = padded_2(solution, (("gx", 2), ("gy", 3)), 1) * unit_mask
            owned_resid = forcing - apply_operator(padded, owned_edges, owned_diag)
            residual_wide = padded_2(owned_resid, (("gx", 2), ("gy", 3)), MARGIN)
            residual_wide = residual_wide * plate_columns(MARGIN, tile_cols)
        residual = residual_wide[:, :, MARGIN:-MARGIN, MARGIN:-MARGIN]
        local_part = local_solve(residual_wide, wide_edges, wide_diag, inside)[
            :, :, MARGIN:-MARGIN, MARGIN:-MARGIN
        ]
        search = lax.all_gather(restrict(residual), ("gx", "gy")).reshape(
            gx_count, gy_count, basis_total, mode_count, 2
        )
        coarse = jnp.zeros_like(search)
        for coarse_step in range(CSTEPS):
            images = coarse_image(search)
            num_real = jnp.sum(
                images[..., 0] * search[..., 0] + images[..., 1] * search[..., 1], axis=(0, 1, 2)
            )
            num_imag = jnp.sum(
                images[..., 0] * search[..., 1] - images[..., 1] * search[..., 0], axis=(0, 1, 2)
            )
            squares = jnp.sum(images * images, axis=(0, 1, 2, 4))
            denominator = squares + guard_value
            alpha_real = num_real / denominator
            alpha_imag = num_imag / denominator
            coarse = coarse + complex_scale(alpha_real, alpha_imag, search)
            search = search - complex_scale(alpha_real, alpha_imag, images)
        own_coarse = coarse[gx_index, gy_index]
        solution = solution + local_part + prolong(own_coarse)
    return solution


def solution(mesh):
    placed = (
        P(None, None, "gx", "gy"),
        P("gx", "gy"),
        P("gx", "gy"),
        P(None, "gx", "gy"),
        P("gx", "gy"),
    )
    return jax.shard_map(
        body, mesh=mesh, in_specs=placed, out_specs=P(None, None, "gx", "gy"), check_vma=False
    )
```

```python
import jax
import jax.numpy as jnp
from jax import lax
from jax.sharding import PartitionSpec as P

MARGIN = 16
SWEEPS = 20
CSTEPS = 7
ITERS = 2


squeeze_number = 0.2
vent_gain = 4.0
relaxation = 0.8
guard_value = 1e-12
highest = lax.Precision.HIGHEST


def padded_2(cells, sides, width):
    for axis, dim in sides:
        count = lax.axis_size(axis)
        head = lax.slice_in_dim(cells, 0, width, axis=dim)
        tail = lax.slice_in_dim(cells, cells.shape[dim] - width, cells.shape[dim], axis=dim)
        cells = jnp.concatenate(
            [
                lax.ppermute(tail, axis, [(i, (i + 1) % count) for i in range(count)]),
                cells,
                lax.ppermute(head, axis, [((i + 1) % count, i) for i in range(count)]),
            ],
            axis=dim,
        )
    return cells


def tree_sum(values, axes):
    for axis in axes:
        count = lax.axis_size(axis)
        if count & (count - 1):
            values = lax.psum(values, axis)
            continue
        stride = 1
        while stride < count:
            values = values + lax.ppermute(values, axis, [(i, i ^ stride) for i in range(count)])
            stride *= 2
    return values


def tree_gather(values, axes):
    for axis in axes:
        count = lax.axis_size(axis)
        if count & (count - 1):
            values = lax.all_gather(values, axis)
            continue
        index = lax.axis_index(axis)
        values = values[None]
        stride = 1
        while stride < count:
            other = lax.ppermute(values, axis, [(i, i ^ stride) for i in range(count)])
            upper = (index // stride) % 2 == 1
            values = jnp.where(upper, jnp.concatenate([other, values]), jnp.concatenate([values, other]))
            stride *= 2
    return values


def edge_terms(gap_padded):
    centre = gap_padded[1:-1, 1:-1]
    north_edge = 0.5 * (centre + gap_padded[2:, 1:-1])
    south_edge = 0.5 * (centre + gap_padded[:-2, 1:-1])
    east_edge = 0.5 * (centre + gap_padded[1:-1, 2:])
    west_edge = 0.5 * (centre + gap_padded[1:-1, :-2])
    return (north_edge, south_edge, east_edge, west_edge)


def diagonal_of(edge_set, vent_term):
    return edge_set[0] + edge_set[1] + edge_set[2] + edge_set[3] + vent_term


def apply_operator(padded, edge_set, diagonal):
    north_edge, south_edge, east_edge, west_edge = edge_set
    centre = padded[:, :, 1:-1, 1:-1]
    beside_all = (
        north_edge * padded[:, :, 2:, 1:-1]
        + south_edge * padded[:, :, :-2, 1:-1]
        + east_edge * padded[:, :, 1:-1, 2:]
        + west_edge * padded[:, :, 1:-1, :-2]
    )
    turned = jnp.stack([-centre[:, 1], centre[:, 0]], axis=1)
    return diagonal * centre - beside_all + squeeze_number * turned


def local_solve(residual, edge_set, diagonal, inside):
    real_diag = jnp.where(inside > 0, diagonal, 1.0)
    step_scale = relaxation * inside / (real_diag * real_diag + squeeze_number * squeeze_number)

    def sweep(sweep_index, iterate):
        padded = jnp.pad(iterate, ((0, 0), (0, 0), (1, 1), (1, 1)))
        defect = residual - apply_operator(padded, edge_set, diagonal)
        update_real = real_diag * defect[:, 0] + squeeze_number * defect[:, 1]
        update_imag = real_diag * defect[:, 1] - squeeze_number * defect[:, 0]
        return iterate + step_scale * jnp.stack([update_real, update_imag], axis=1)

    return lax.fori_loop(0, SWEEPS, sweep, jnp.zeros_like(residual))


def complex_scale(alpha_real, alpha_imag, vectors):
    return jnp.stack(
        [
            alpha_real * vectors[..., 0] - alpha_imag * vectors[..., 1],
            alpha_real * vectors[..., 1] + alpha_imag * vectors[..., 0],
        ],
        axis=-1,
    )


def plate_columns(width, tile_cols):
    first_col = lax.axis_index("gy") * tile_cols - width
    col_ids = first_col + jnp.arange(tile_cols + 2 * width, dtype=jnp.int32)
    return ((col_ids >= 0) & (col_ids < tile_cols * lax.axis_size("gy"))).astype(jnp.float32)


def body(forcing, gap_cubed, hole_mask, coarse_bases, basis_counts):
    mode_count = forcing.shape[0]
    tile_rows, tile_cols = gap_cubed.shape
    basis_total = coarse_bases.shape[0]
    deep_width = MARGIN + 1
    wide_rows = tile_rows + 2 * MARGIN
    wide_cols = tile_cols + 2 * MARGIN
    vent_term = vent_gain * hole_mask.astype(jnp.float32) * gap_cubed
    start_stack = jnp.concatenate(
        [gap_cubed[None], vent_term[None], forcing.reshape(2 * mode_count, tile_rows, tile_cols)],
        axis=0,
    )
    grown_stack = padded_2(start_stack, (("gx", 1), ("gy", 2)), deep_width)
    grown_stack = grown_stack * plate_columns(deep_width, tile_cols)
    gap_deep = grown_stack[0]
    vent_wide = grown_stack[1, 1:-1, 1:-1]
    force_wide = grown_stack[2:, 1:-1, 1:-1].reshape(mode_count, 2, wide_rows, wide_cols)
    inside = jnp.broadcast_to(plate_columns(MARGIN, tile_cols)[None, :], (wide_rows, wide_cols))
    wide_edges = edge_terms(gap_deep)
    wide_diag = diagonal_of(wide_edges, vent_wide)
    owned_edges = edge_terms(gap_deep[MARGIN:-MARGIN, MARGIN:-MARGIN])
    owned_diag = diagonal_of(owned_edges, vent_term)
    unit_mask = plate_columns(1, tile_cols)
    active = (jnp.arange(basis_total, dtype=jnp.int32) < basis_counts[0, 0]).astype(jnp.float32)
    base_field = coarse_bases * active[:, None, None]
    flat_bases = base_field.reshape(basis_total, tile_rows * tile_cols)

    def restrict(pressure):
        flat_field = pressure.reshape(2 * mode_count, tile_rows * tile_cols)
        product = lax.dot_general(
            flat_bases,
            flat_field,
            (((1,), (1,)), ((), ())),
            precision=highest,
            preferred_element_type=jnp.float32,
        )
        return product.reshape(basis_total, mode_count, 2)

    def prolong(coarse):
        product = lax.dot_general(
            coarse.reshape(basis_total, 2 * mode_count),
            flat_bases,
            (((0,), (0,)), ((), ())),
            precision=highest,
            preferred_element_type=jnp.float32,
        )
        return product.reshape(mode_count, 2, tile_rows, tile_cols)

    def pair(left, right):
        return lax.dot_general(
            left, right, (((1,), (1,)), ((), ())), precision=highest, preferred_element_type=jnp.float32
        )

    gx_count = lax.axis_size("gx")
    gy_count = lax.axis_size("gy")
    gy_index = lax.axis_index("gy")
    north_edge, south_edge, east_edge, west_edge = owned_edges
    from_next_x = lax.ppermute(base_field[:, 0, :], "gx", [((i + 1) % gx_count, i) for i in range(gx_count)])
    from_prev_x = lax.ppermute(base_field[:, -1, :], "gx", [(i, (i + 1) % gx_count) for i in range(gx_count)])
    from_next_y = lax.ppermute(base_field[:, :, 0], "gy", [((i + 1) % gy_count, i) for i in range(gy_count)])
    from_prev_y = lax.ppermute(base_field[:, :, -1], "gy", [(i, (i + 1) % gy_count) for i in range(gy_count)])
    has_next_y = (gy_index < gy_count - 1).astype(jnp.float32)
    has_prev_y = (gy_index > 0).astype(jnp.float32)
    base_padded = jnp.pad(base_field, ((0, 0), (1, 1), (1, 1)))
    base_image = owned_diag * base_field - (
        north_edge * base_padded[:, 2:, 1:-1]
        + south_edge * base_padded[:, :-2, 1:-1]
        + east_edge * base_padded[:, 1:-1, 2:]
        + west_edge * base_padded[:, 1:-1, :-2]
    )
    self_block = pair(flat_bases, base_image.reshape(basis_total, tile_rows * tile_cols))
    gram_block = pair(flat_bases, flat_bases)
    next_x_block = -pair(base_field[:, -1, :] * north_edge[-1], from_next_x)
    prev_x_block = -pair(base_field[:, 0, :] * south_edge[0], from_prev_x)
    next_y_block = -pair(base_field[:, :, -1] * east_edge[:, -1], from_next_y) * has_next_y
    prev_y_block = -pair(base_field[:, :, 0] * west_edge[:, 0], from_prev_y) * has_prev_y
    block_set = jnp.stack(
        [self_block, next_x_block, prev_x_block, next_y_block, prev_y_block, squeeze_number * gram_block]
    )
    tile_total = gx_count * gy_count
    all_blocks = jnp.moveaxis(lax.all_gather(block_set, ("gx", "gy")), 0, -1)

    def coarse_image(search):
        halves = search.reshape(basis_total, mode_count, 2, tile_total)
        turned = jnp.stack([-halves[:, :, 1], halves[:, :, 0]], axis=2).reshape(search.shape)
        shifted = (
            search,
            jnp.roll(search, -gy_count, axis=-1),
            jnp.roll(search, gy_count, axis=-1),
            jnp.roll(search, -1, axis=-1),
            jnp.roll(search, 1, axis=-1),
            turned,
        )
        total = None
        for block, vectors in zip(all_blocks, shifted):
            term = jnp.sum(block[:, :, None, :] * vectors[None, :, :, :], axis=1)
            total = term if total is None else total + term
        return total

    gx_index = lax.axis_index("gx")
    tile_index = gx_index * gy_count + gy_index
    solution = jnp.zeros_like(forcing)
    residual_wide = force_wide
    for outer_step in range(ITERS):
        if outer_step > 0:
            padded = padded_2(solution, (("gx", 2), ("gy", 3)), 1) * unit_mask
            owned_resid = forcing - apply_operator(padded, owned_edges, owned_diag)
            residual_wide = padded_2(owned_resid, (("gx", 2), ("gy", 3)), MARGIN)
            residual_wide = residual_wide * plate_columns(MARGIN, tile_cols)
        residual = residual_wide[:, :, MARGIN:-MARGIN, MARGIN:-MARGIN]
        local_part = local_solve(residual_wide, wide_edges, wide_diag, inside)[
            :, :, MARGIN:-MARGIN, MARGIN:-MARGIN
        ]
        gathered = tree_gather(restrict(residual).reshape(-1), ("gy", "gx"))
        search = gathered.reshape(tile_total, -1).T.reshape(basis_total, 2 * mode_count, tile_total)
        coarse = jnp.zeros_like(search)
        for coarse_step in range(CSTEPS):
            images = coarse_image(search)
            image_halves = images.reshape(basis_total, mode_count, 2, tile_total)
            search_halves = search.reshape(basis_total, mode_count, 2, tile_total)
            num_real = jnp.sum(
                image_halves[:, :, 0] * search_halves[:, :, 0] + image_halves[:, :, 1] * search_halves[:, :, 1],
                axis=(0, 2),
            )
            num_imag = jnp.sum(
                image_halves[:, :, 0] * search_halves[:, :, 1] - image_halves[:, :, 1] * search_halves[:, :, 0],
                axis=(0, 2),
            )
            squares = jnp.sum(image_halves * image_halves, axis=(0, 2, 3))
            denominator = squares + guard_value
            alpha_real = (num_real / denominator)[None, :, None]
            alpha_imag = (num_imag / denominator)[None, :, None]
            coarse_halves = coarse.reshape(search_halves.shape)
            coarse = jnp.stack(
                [
                    coarse_halves[:, :, 0] + alpha_real * search_halves[:, :, 0] - alpha_imag * search_halves[:, :, 1],
                    coarse_halves[:, :, 1] + alpha_real * search_halves[:, :, 1] + alpha_imag * search_halves[:, :, 0],
                ],
                axis=2,
            ).reshape(search.shape)
            search = jnp.stack(
                [
                    search_halves[:, :, 0] - (alpha_real * image_halves[:, :, 0] - alpha_imag * image_halves[:, :, 1]),
                    search_halves[:, :, 1] - (alpha_real * image_halves[:, :, 1] + alpha_imag * image_halves[:, :, 0]),
                ],
                axis=2,
            ).reshape(search.shape)
        own_coarse = lax.dynamic_index_in_dim(coarse, tile_index, axis=2, keepdims=False)
        solution = solution + local_part + prolong(own_coarse)
    return solution


def solution(mesh):
    placed = (
        P(None, None, "gx", "gy"),
        P("gx", "gy"),
        P("gx", "gy"),
        P(None, "gx", "gy"),
        P("gx", "gy"),
    )
    return jax.shard_map(
        body, mesh=mesh, in_specs=placed, out_specs=P(None, None, "gx", "gy"), check_vma=False
    )
```

```python
import jax
import jax.numpy as jnp
from jax import lax
from jax.sharding import PartitionSpec as P

MARGIN = 16
SWEEPS = 20
CSTEPS = 7
ITERS = 2


squeeze_number = 0.2
vent_gain = 4.0
relaxation = 0.8
guard_value = 1e-12
highest = lax.Precision.HIGHEST


def padded_2(cells, sides, width):
    for axis, dim in sides:
        count = lax.axis_size(axis)
        head = lax.slice_in_dim(cells, 0, width, axis=dim)
        tail = lax.slice_in_dim(cells, cells.shape[dim] - width, cells.shape[dim], axis=dim)
        cells = jnp.concatenate(
            [
                lax.ppermute(tail, axis, [(i, (i + 1) % count) for i in range(count)]),
                cells,
                lax.ppermute(head, axis, [((i + 1) % count, i) for i in range(count)]),
            ],
            axis=dim,
        )
    return cells


def tree_sum(values, axes):
    for axis in axes:
        count = lax.axis_size(axis)
        if count & (count - 1):
            values = lax.psum(values, axis)
            continue
        stride = 1
        while stride < count:
            values = values + lax.ppermute(values, axis, [(i, i ^ stride) for i in range(count)])
            stride *= 2
    return values


def tree_gather(values, axes):
    for axis in axes:
        count = lax.axis_size(axis)
        if count & (count - 1):
            values = lax.all_gather(values, axis)
            continue
        index = lax.axis_index(axis)
        values = values[None]
        stride = 1
        while stride < count:
            other = lax.ppermute(values, axis, [(i, i ^ stride) for i in range(count)])
            upper = (index // stride) % 2 == 1
            values = jnp.where(upper, jnp.concatenate([other, values]), jnp.concatenate([values, other]))
            stride *= 2
    return values


def edge_terms(gap_padded):
    centre = gap_padded[1:-1, 1:-1]
    north_edge = 0.5 * (centre + gap_padded[2:, 1:-1])
    south_edge = 0.5 * (centre + gap_padded[:-2, 1:-1])
    east_edge = 0.5 * (centre + gap_padded[1:-1, 2:])
    west_edge = 0.5 * (centre + gap_padded[1:-1, :-2])
    return (north_edge, south_edge, east_edge, west_edge)


def diagonal_of(edge_set, vent_term):
    return edge_set[0] + edge_set[1] + edge_set[2] + edge_set[3] + vent_term


def apply_operator(padded, edge_set, diagonal):
    north_edge, south_edge, east_edge, west_edge = edge_set
    centre = padded[:, :, 1:-1, 1:-1]
    beside_all = (
        north_edge * padded[:, :, 2:, 1:-1]
        + south_edge * padded[:, :, :-2, 1:-1]
        + east_edge * padded[:, :, 1:-1, 2:]
        + west_edge * padded[:, :, 1:-1, :-2]
    )
    turned = jnp.stack([-centre[:, 1], centre[:, 0]], axis=1)
    return diagonal * centre - beside_all + squeeze_number * turned


def local_solve(residual, edge_set, diagonal, inside):
    real_diag = jnp.where(inside > 0, diagonal, 1.0)
    step_scale = relaxation * inside / (real_diag * real_diag + squeeze_number * squeeze_number)

    def sweep(sweep_index, iterate):
        padded = jnp.pad(iterate, ((0, 0), (0, 0), (1, 1), (1, 1)))
        defect = residual - apply_operator(padded, edge_set, diagonal)
        update_real = real_diag * defect[:, 0] + squeeze_number * defect[:, 1]
        update_imag = real_diag * defect[:, 1] - squeeze_number * defect[:, 0]
        return iterate + step_scale * jnp.stack([update_real, update_imag], axis=1)

    return lax.fori_loop(0, SWEEPS, sweep, jnp.zeros_like(residual))


def complex_scale(alpha_real, alpha_imag, vectors):
    return jnp.stack(
        [
            alpha_real * vectors[..., 0] - alpha_imag * vectors[..., 1],
            alpha_real * vectors[..., 1] + alpha_imag * vectors[..., 0],
        ],
        axis=-1,
    )


def plate_columns(width, tile_cols):
    first_col = lax.axis_index("gy") * tile_cols - width
    col_ids = first_col + jnp.arange(tile_cols + 2 * width, dtype=jnp.int32)
    return ((col_ids >= 0) & (col_ids < tile_cols * lax.axis_size("gy"))).astype(jnp.float32)


def body(forcing, gap_cubed, hole_mask, coarse_bases, basis_counts):
    mode_count = forcing.shape[0]
    tile_rows, tile_cols = gap_cubed.shape
    basis_total = coarse_bases.shape[0]
    deep_width = MARGIN + 1
    wide_rows = tile_rows + 2 * MARGIN
    wide_cols = tile_cols + 2 * MARGIN
    vent_term = vent_gain * hole_mask.astype(jnp.float32) * gap_cubed
    start_stack = jnp.concatenate(
        [gap_cubed[None], vent_term[None], forcing.reshape(2 * mode_count, tile_rows, tile_cols)],
        axis=0,
    )
    grown_stack = padded_2(start_stack, (("gx", 1), ("gy", 2)), deep_width)
    grown_stack = grown_stack * plate_columns(deep_width, tile_cols)
    gap_deep = grown_stack[0]
    vent_wide = grown_stack[1, 1:-1, 1:-1]
    force_wide = grown_stack[2:, 1:-1, 1:-1].reshape(mode_count, 2, wide_rows, wide_cols)
    inside = jnp.broadcast_to(plate_columns(MARGIN, tile_cols)[None, :], (wide_rows, wide_cols))
    wide_edges = edge_terms(gap_deep)
    wide_diag = diagonal_of(wide_edges, vent_wide)
    owned_edges = edge_terms(gap_deep[MARGIN:-MARGIN, MARGIN:-MARGIN])
    owned_diag = diagonal_of(owned_edges, vent_term)
    unit_mask = plate_columns(1, tile_cols)
    active = (jnp.arange(basis_total, dtype=jnp.int32) < basis_counts[0, 0]).astype(jnp.float32)
    base_field = coarse_bases * active[:, None, None]
    flat_bases = base_field.reshape(basis_total, tile_rows * tile_cols)

    def restrict(pressure):
        flat_field = pressure.reshape(2 * mode_count, tile_rows * tile_cols)
        product = lax.dot_general(
            flat_bases,
            flat_field,
            (((1,), (1,)), ((), ())),
            precision=highest,
            preferred_element_type=jnp.float32,
        )
        return product.reshape(basis_total, mode_count, 2)

    def prolong(coarse):
        product = lax.dot_general(
            coarse.reshape(basis_total, 2 * mode_count),
            flat_bases,
            (((0,), (0,)), ((), ())),
            precision=highest,
            preferred_element_type=jnp.float32,
        )
        return product.reshape(mode_count, 2, tile_rows, tile_cols)

    def pair(left, right):
        return lax.dot_general(
            left, right, (((1,), (1,)), ((), ())), precision=highest, preferred_element_type=jnp.float32
        )

    gx_count = lax.axis_size("gx")
    gy_count = lax.axis_size("gy")
    gy_index = lax.axis_index("gy")
    north_edge, south_edge, east_edge, west_edge = owned_edges
    from_next_x = lax.ppermute(base_field[:, 0, :], "gx", [((i + 1) % gx_count, i) for i in range(gx_count)])
    from_prev_x = lax.ppermute(base_field[:, -1, :], "gx", [(i, (i + 1) % gx_count) for i in range(gx_count)])
    from_next_y = lax.ppermute(base_field[:, :, 0], "gy", [((i + 1) % gy_count, i) for i in range(gy_count)])
    from_prev_y = lax.ppermute(base_field[:, :, -1], "gy", [(i, (i + 1) % gy_count) for i in range(gy_count)])
    has_next_y = (gy_index < gy_count - 1).astype(jnp.float32)
    has_prev_y = (gy_index > 0).astype(jnp.float32)
    base_padded = jnp.pad(base_field, ((0, 0), (1, 1), (1, 1)))
    base_image = owned_diag * base_field - (
        north_edge * base_padded[:, 2:, 1:-1]
        + south_edge * base_padded[:, :-2, 1:-1]
        + east_edge * base_padded[:, 1:-1, 2:]
        + west_edge * base_padded[:, 1:-1, :-2]
    )
    self_block = pair(flat_bases, base_image.reshape(basis_total, tile_rows * tile_cols))
    gram_block = pair(flat_bases, flat_bases)
    next_x_block = -pair(base_field[:, -1, :] * north_edge[-1], from_next_x)
    prev_x_block = -pair(base_field[:, 0, :] * south_edge[0], from_prev_x)
    next_y_block = -pair(base_field[:, :, -1] * east_edge[:, -1], from_next_y) * has_next_y
    prev_y_block = -pair(base_field[:, :, 0] * west_edge[:, 0], from_prev_y) * has_prev_y
    block_set = jnp.stack(
        [self_block, next_x_block, prev_x_block, next_y_block, prev_y_block, squeeze_number * gram_block]
    )
    tile_total = gx_count * gy_count
    all_blocks = lax.all_gather(block_set, ("gx", "gy"), axis=3)

    def coarse_image(search):
        halves = search.reshape(basis_total, mode_count, 2, tile_total)
        turned = jnp.stack([-halves[:, :, 1], halves[:, :, 0]], axis=2).reshape(search.shape)
        shifted = (
            search,
            jnp.roll(search, -gy_count, axis=-1),
            jnp.roll(search, gy_count, axis=-1),
            jnp.roll(search, -1, axis=-1),
            jnp.roll(search, 1, axis=-1),
            turned,
        )
        total = None
        for block, vectors in zip(all_blocks, shifted):
            term = jnp.sum(block[:, :, None, :] * vectors[None, :, :, :], axis=1)
            total = term if total is None else total + term
        return total

    gx_index = lax.axis_index("gx")
    tile_index = gx_index * gy_count + gy_index
    solution = jnp.zeros_like(forcing)
    residual_wide = force_wide
    for outer_step in range(ITERS):
        if outer_step > 0:
            solution_deep = padded_2(solution, (("gx", 2), ("gy", 3)), deep_width) * plate_columns(deep_width, tile_cols)
            residual_wide = force_wide - apply_operator(solution_deep, wide_edges, wide_diag)
            residual_wide = residual_wide * plate_columns(MARGIN, tile_cols)
        residual = residual_wide[:, :, MARGIN:-MARGIN, MARGIN:-MARGIN]
        local_part = local_solve(residual_wide, wide_edges, wide_diag, inside)[
            :, :, MARGIN:-MARGIN, MARGIN:-MARGIN
        ]
        gathered = tree_gather(restrict(residual).reshape(-1), ("gy", "gx"))
        search = gathered.reshape(tile_total, -1).T.reshape(basis_total, 2 * mode_count, tile_total)
        coarse = jnp.zeros_like(search)
        for coarse_step in range(CSTEPS):
            images = coarse_image(search)
            image_halves = images.reshape(basis_total, mode_count, 2, tile_total)
            search_halves = search.reshape(basis_total, mode_count, 2, tile_total)
            num_real = jnp.sum(
                image_halves[:, :, 0] * search_halves[:, :, 0] + image_halves[:, :, 1] * search_halves[:, :, 1],
                axis=(0, 2),
            )
            num_imag = jnp.sum(
                image_halves[:, :, 0] * search_halves[:, :, 1] - image_halves[:, :, 1] * search_halves[:, :, 0],
                axis=(0, 2),
            )
            squares = jnp.sum(image_halves * image_halves, axis=(0, 2, 3))
            denominator = squares + guard_value
            alpha_real = (num_real / denominator)[None, :, None]
            alpha_imag = (num_imag / denominator)[None, :, None]
            coarse_halves = coarse.reshape(search_halves.shape)
            coarse = jnp.stack(
                [
                    coarse_halves[:, :, 0] + alpha_real * search_halves[:, :, 0] - alpha_imag * search_halves[:, :, 1],
                    coarse_halves[:, :, 1] + alpha_real * search_halves[:, :, 1] + alpha_imag * search_halves[:, :, 0],
                ],
                axis=2,
            ).reshape(search.shape)
            search = jnp.stack(
                [
                    search_halves[:, :, 0] - (alpha_real * image_halves[:, :, 0] - alpha_imag * image_halves[:, :, 1]),
                    search_halves[:, :, 1] - (alpha_real * image_halves[:, :, 1] + alpha_imag * image_halves[:, :, 0]),
                ],
                axis=2,
            ).reshape(search.shape)
        own_coarse = lax.dynamic_index_in_dim(coarse, tile_index, axis=2, keepdims=False)
        solution = solution + local_part + prolong(own_coarse)
    return solution


def solution(mesh):
    placed = (
        P(None, None, "gx", "gy"),
        P("gx", "gy"),
        P("gx", "gy"),
        P(None, "gx", "gy"),
        P("gx", "gy"),
    )
    return jax.shard_map(
        body, mesh=mesh, in_specs=placed, out_specs=P(None, None, "gx", "gy"), check_vma=False
    )
```

```python
import jax
import jax.numpy as jnp
from jax import lax
from jax.sharding import PartitionSpec as P

MARGIN = 16
SWEEPS = 20
CSTEPS = 7
ITERS = 2


squeeze_number = 0.2
vent_gain = 4.0
relaxation = 0.8
guard_value = 1e-12
highest = lax.Precision.HIGHEST


def padded_2(cells, sides, width):
    for axis, dim in sides:
        count = lax.axis_size(axis)
        head = lax.slice_in_dim(cells, 0, width, axis=dim)
        tail = lax.slice_in_dim(cells, cells.shape[dim] - width, cells.shape[dim], axis=dim)
        cells = jnp.concatenate(
            [
                lax.ppermute(tail, axis, [(i, (i + 1) % count) for i in range(count)]),
                cells,
                lax.ppermute(head, axis, [((i + 1) % count, i) for i in range(count)]),
            ],
            axis=dim,
        )
    return cells


def tree_sum(values, axes):
    for axis in axes:
        count = lax.axis_size(axis)
        if count & (count - 1):
            values = lax.psum(values, axis)
            continue
        stride = 1
        while stride < count:
            values = values + lax.ppermute(values, axis, [(i, i ^ stride) for i in range(count)])
            stride *= 2
    return values


def tree_gather(values, axes):
    for axis in axes:
        count = lax.axis_size(axis)
        if count & (count - 1):
            values = lax.all_gather(values, axis)
            continue
        index = lax.axis_index(axis)
        values = values[None]
        stride = 1
        while stride < count:
            other = lax.ppermute(values, axis, [(i, i ^ stride) for i in range(count)])
            upper = (index // stride) % 2 == 1
            values = jnp.where(upper, jnp.concatenate([other, values]), jnp.concatenate([values, other]))
            stride *= 2
    return values


def edge_terms(gap_padded):
    centre = gap_padded[1:-1, 1:-1]
    north_edge = 0.5 * (centre + gap_padded[2:, 1:-1])
    south_edge = 0.5 * (centre + gap_padded[:-2, 1:-1])
    east_edge = 0.5 * (centre + gap_padded[1:-1, 2:])
    west_edge = 0.5 * (centre + gap_padded[1:-1, :-2])
    return (north_edge, south_edge, east_edge, west_edge)


def diagonal_of(edge_set, vent_term):
    return edge_set[0] + edge_set[1] + edge_set[2] + edge_set[3] + vent_term


def apply_operator(padded, edge_set, diagonal):
    north_edge, south_edge, east_edge, west_edge = edge_set
    centre = padded[:, :, 1:-1, 1:-1]
    beside_all = (
        north_edge * padded[:, :, 2:, 1:-1]
        + south_edge * padded[:, :, :-2, 1:-1]
        + east_edge * padded[:, :, 1:-1, 2:]
        + west_edge * padded[:, :, 1:-1, :-2]
    )
    turned = jnp.stack([-centre[:, 1], centre[:, 0]], axis=1)
    return diagonal * centre - beside_all + squeeze_number * turned


def local_solve(residual, edge_set, diagonal, inside):
    real_diag = jnp.where(inside > 0, diagonal, 1.0)
    step_scale = relaxation * inside / (real_diag * real_diag + squeeze_number * squeeze_number)

    def sweep(sweep_index, iterate):
        padded = jnp.pad(iterate, ((0, 0), (0, 0), (1, 1), (1, 1)))
        defect = residual - apply_operator(padded, edge_set, diagonal)
        update_real = real_diag * defect[:, 0] + squeeze_number * defect[:, 1]
        update_imag = real_diag * defect[:, 1] - squeeze_number * defect[:, 0]
        return iterate + step_scale * jnp.stack([update_real, update_imag], axis=1)

    return lax.fori_loop(0, SWEEPS, sweep, jnp.zeros_like(residual))


def complex_scale(alpha_real, alpha_imag, vectors):
    return jnp.stack(
        [
            alpha_real * vectors[..., 0] - alpha_imag * vectors[..., 1],
            alpha_real * vectors[..., 1] + alpha_imag * vectors[..., 0],
        ],
        axis=-1,
    )


def plate_columns(width, tile_cols):
    first_col = lax.axis_index("gy") * tile_cols - width
    col_ids = first_col + jnp.arange(tile_cols + 2 * width, dtype=jnp.int32)
    return ((col_ids >= 0) & (col_ids < tile_cols * lax.axis_size("gy"))).astype(jnp.float32)


def body(forcing, gap_cubed, hole_mask, coarse_bases, basis_counts):
    mode_count = forcing.shape[0]
    tile_rows, tile_cols = gap_cubed.shape
    basis_total = coarse_bases.shape[0]
    deep_width = MARGIN + 1
    wide_rows = tile_rows + 2 * MARGIN
    wide_cols = tile_cols + 2 * MARGIN
    vent_term = vent_gain * hole_mask.astype(jnp.float32) * gap_cubed
    start_stack = jnp.concatenate(
        [gap_cubed[None], vent_term[None], forcing.reshape(2 * mode_count, tile_rows, tile_cols)],
        axis=0,
    )
    grown_stack = padded_2(start_stack, (("gx", 1), ("gy", 2)), deep_width)
    grown_stack = grown_stack * plate_columns(deep_width, tile_cols)
    gap_deep = grown_stack[0]
    vent_wide = grown_stack[1, 1:-1, 1:-1]
    force_wide = grown_stack[2:, 1:-1, 1:-1].reshape(mode_count, 2, wide_rows, wide_cols)
    inside = jnp.broadcast_to(plate_columns(MARGIN, tile_cols)[None, :], (wide_rows, wide_cols))
    wide_edges = edge_terms(gap_deep)
    wide_diag = diagonal_of(wide_edges, vent_wide)
    owned_edges = edge_terms(gap_deep[MARGIN:-MARGIN, MARGIN:-MARGIN])
    owned_diag = diagonal_of(owned_edges, vent_term)
    unit_mask = plate_columns(1, tile_cols)
    active = (jnp.arange(basis_total, dtype=jnp.int32) < basis_counts[0, 0]).astype(jnp.float32)
    base_field = coarse_bases * active[:, None, None]
    flat_bases = base_field.reshape(basis_total, tile_rows * tile_cols)

    def restrict(pressure):
        flat_field = pressure.reshape(2 * mode_count, tile_rows * tile_cols)
        product = lax.dot_general(
            flat_bases,
            flat_field,
            (((1,), (1,)), ((), ())),
            precision=highest,
            preferred_element_type=jnp.float32,
        )
        return product.reshape(basis_total, mode_count, 2)

    def prolong(coarse):
        product = lax.dot_general(
            coarse.reshape(basis_total, 2 * mode_count),
            flat_bases,
            (((0,), (0,)), ((), ())),
            precision=highest,
            preferred_element_type=jnp.float32,
        )
        return product.reshape(mode_count, 2, tile_rows, tile_cols)

    def pair(left, right):
        return lax.dot_general(
            left, right, (((1,), (1,)), ((), ())), precision=highest, preferred_element_type=jnp.float32
        )

    gx_count = lax.axis_size("gx")
    gy_count = lax.axis_size("gy")
    gy_index = lax.axis_index("gy")
    north_edge, south_edge, east_edge, west_edge = owned_edges
    from_next_x = lax.ppermute(base_field[:, 0, :], "gx", [((i + 1) % gx_count, i) for i in range(gx_count)])
    from_prev_x = lax.ppermute(base_field[:, -1, :], "gx", [(i, (i + 1) % gx_count) for i in range(gx_count)])
    from_next_y = lax.ppermute(base_field[:, :, 0], "gy", [((i + 1) % gy_count, i) for i in range(gy_count)])
    from_prev_y = lax.ppermute(base_field[:, :, -1], "gy", [(i, (i + 1) % gy_count) for i in range(gy_count)])
    has_next_y = (gy_index < gy_count - 1).astype(jnp.float32)
    has_prev_y = (gy_index > 0).astype(jnp.float32)
    base_padded = jnp.pad(base_field, ((0, 0), (1, 1), (1, 1)))
    base_image = owned_diag * base_field - (
        north_edge * base_padded[:, 2:, 1:-1]
        + south_edge * base_padded[:, :-2, 1:-1]
        + east_edge * base_padded[:, 1:-1, 2:]
        + west_edge * base_padded[:, 1:-1, :-2]
    )
    self_block = pair(flat_bases, base_image.reshape(basis_total, tile_rows * tile_cols))
    gram_block = pair(flat_bases, flat_bases)
    next_x_block = -pair(base_field[:, -1, :] * north_edge[-1], from_next_x)
    prev_x_block = -pair(base_field[:, 0, :] * south_edge[0], from_prev_x)
    next_y_block = -pair(base_field[:, :, -1] * east_edge[:, -1], from_next_y) * has_next_y
    prev_y_block = -pair(base_field[:, :, 0] * west_edge[:, 0], from_prev_y) * has_prev_y
    block_set = jnp.stack(
        [self_block, next_x_block, prev_x_block, next_y_block, prev_y_block, squeeze_number * gram_block]
    )
    tile_total = gx_count * gy_count
    gathered_blocks = lax.all_gather(block_set.reshape(1, -1), ("gx", "gy"), axis=0, tiled=True)
    all_blocks = gathered_blocks.T.reshape(block_set.shape + (tile_total,))

    def coarse_image(search):
        halves = search.reshape(basis_total, mode_count, 2, tile_total)
        turned = jnp.stack([-halves[:, :, 1], halves[:, :, 0]], axis=2).reshape(search.shape)
        shifted = (
            search,
            jnp.roll(search, -gy_count, axis=-1),
            jnp.roll(search, gy_count, axis=-1),
            jnp.roll(search, -1, axis=-1),
            jnp.roll(search, 1, axis=-1),
            turned,
        )
        total = None
        for block, vectors in zip(all_blocks, shifted):
            term = jnp.sum(block[:, :, None, :] * vectors[None, :, :, :], axis=1)
            total = term if total is None else total + term
        return total

    gx_index = lax.axis_index("gx")
    tile_index = gx_index * gy_count + gy_index
    solution = jnp.zeros_like(forcing)
    residual_wide = force_wide
    for outer_step in range(ITERS):
        if outer_step > 0:
            solution_deep = padded_2(solution, (("gx", 2), ("gy", 3)), deep_width) * plate_columns(deep_width, tile_cols)
            residual_wide = force_wide - apply_operator(solution_deep, wide_edges, wide_diag)
            residual_wide = residual_wide * plate_columns(MARGIN, tile_cols)
        residual = residual_wide[:, :, MARGIN:-MARGIN, MARGIN:-MARGIN]
        local_part = local_solve(residual_wide, wide_edges, wide_diag, inside)[
            :, :, MARGIN:-MARGIN, MARGIN:-MARGIN
        ]
        gathered = tree_gather(restrict(residual).reshape(-1), ("gy", "gx"))
        search = gathered.reshape(tile_total, -1).T.reshape(basis_total, 2 * mode_count, tile_total)
        coarse = jnp.zeros_like(search)
        for coarse_step in range(CSTEPS):
            images = coarse_image(search)
            image_halves = images.reshape(basis_total, mode_count, 2, tile_total)
            search_halves = search.reshape(basis_total, mode_count, 2, tile_total)
            num_real = jnp.sum(
                image_halves[:, :, 0] * search_halves[:, :, 0] + image_halves[:, :, 1] * search_halves[:, :, 1],
                axis=(0, 2),
            )
            num_imag = jnp.sum(
                image_halves[:, :, 0] * search_halves[:, :, 1] - image_halves[:, :, 1] * search_halves[:, :, 0],
                axis=(0, 2),
            )
            squares = jnp.sum(image_halves * image_halves, axis=(0, 2, 3))
            denominator = squares + guard_value
            alpha_real = (num_real / denominator)[None, :, None]
            alpha_imag = (num_imag / denominator)[None, :, None]
            coarse_halves = coarse.reshape(search_halves.shape)
            coarse = jnp.stack(
                [
                    coarse_halves[:, :, 0] + alpha_real * search_halves[:, :, 0] - alpha_imag * search_halves[:, :, 1],
                    coarse_halves[:, :, 1] + alpha_real * search_halves[:, :, 1] + alpha_imag * search_halves[:, :, 0],
                ],
                axis=2,
            ).reshape(search.shape)
            search = jnp.stack(
                [
                    search_halves[:, :, 0] - (alpha_real * image_halves[:, :, 0] - alpha_imag * image_halves[:, :, 1]),
                    search_halves[:, :, 1] - (alpha_real * image_halves[:, :, 1] + alpha_imag * image_halves[:, :, 0]),
                ],
                axis=2,
            ).reshape(search.shape)
        own_coarse = lax.dynamic_index_in_dim(coarse, tile_index, axis=2, keepdims=False)
        solution = solution + local_part + prolong(own_coarse)
    return solution


def solution(mesh):
    placed = (
        P(None, None, "gx", "gy"),
        P("gx", "gy"),
        P("gx", "gy"),
        P(None, "gx", "gy"),
        P("gx", "gy"),
    )
    return jax.shard_map(
        body, mesh=mesh, in_specs=placed, out_specs=P(None, None, "gx", "gy"), check_vma=False
    )
```

```python
import jax
import jax.numpy as jnp
from jax import lax
from jax.experimental import pallas as pl
from jax.experimental.pallas import tpu as pltpu
from jax.sharding import PartitionSpec as P

MARGIN = 16
SWEEPS = 20
CSTEPS = 7
ITERS = 2


squeeze_number = 0.2
vent_gain = 4.0
relaxation = 0.8
guard_value = 1e-12
highest = lax.Precision.HIGHEST


def padded_2(cells, sides, width):
    for axis, dim in sides:
        count = lax.axis_size(axis)
        head = lax.slice_in_dim(cells, 0, width, axis=dim)
        tail = lax.slice_in_dim(cells, cells.shape[dim] - width, cells.shape[dim], axis=dim)
        cells = jnp.concatenate(
            [
                lax.ppermute(tail, axis, [(i, (i + 1) % count) for i in range(count)]),
                cells,
                lax.ppermute(head, axis, [((i + 1) % count, i) for i in range(count)]),
            ],
            axis=dim,
        )
    return cells


def tree_sum(values, axes):
    for axis in axes:
        count = lax.axis_size(axis)
        if count & (count - 1):
            values = lax.psum(values, axis)
            continue
        stride = 1
        while stride < count:
            values = values + lax.ppermute(values, axis, [(i, i ^ stride) for i in range(count)])
            stride *= 2
    return values


def tree_gather(values, axes):
    for axis in axes:
        count = lax.axis_size(axis)
        if count & (count - 1):
            values = lax.all_gather(values, axis)
            continue
        index = lax.axis_index(axis)
        values = values[None]
        stride = 1
        while stride < count:
            other = lax.ppermute(values, axis, [(i, i ^ stride) for i in range(count)])
            upper = (index // stride) % 2 == 1
            values = jnp.where(upper, jnp.concatenate([other, values]), jnp.concatenate([values, other]))
            stride *= 2
    return values


def edge_terms(gap_padded):
    centre = gap_padded[1:-1, 1:-1]
    north_edge = 0.5 * (centre + gap_padded[2:, 1:-1])
    south_edge = 0.5 * (centre + gap_padded[:-2, 1:-1])
    east_edge = 0.5 * (centre + gap_padded[1:-1, 2:])
    west_edge = 0.5 * (centre + gap_padded[1:-1, :-2])
    return (north_edge, south_edge, east_edge, west_edge)


def diagonal_of(edge_set, vent_term):
    return edge_set[0] + edge_set[1] + edge_set[2] + edge_set[3] + vent_term


def apply_operator(padded, edge_set, diagonal):
    north_edge, south_edge, east_edge, west_edge = edge_set
    centre = padded[:, :, 1:-1, 1:-1]
    beside_all = (
        north_edge * padded[:, :, 2:, 1:-1]
        + south_edge * padded[:, :, :-2, 1:-1]
        + east_edge * padded[:, :, 1:-1, 2:]
        + west_edge * padded[:, :, 1:-1, :-2]
    )
    turned = jnp.stack([-centre[:, 1], centre[:, 0]], axis=1)
    return diagonal * centre - beside_all + squeeze_number * turned


INTERPRET = False


def sweep_kernel(resid_ref, north_ref, south_ref, east_ref, west_ref, diag_ref, real_ref, scale_ref, out_ref):
    pairs, _, rows, lanes = out_ref.shape
    out_ref[...] = jnp.zeros(out_ref.shape, jnp.float32)

    def sweep(sweep_index, carry):
        for pair_index in range(pairs):
            centre_real = out_ref[pair_index, 0]
            centre_imag = out_ref[pair_index, 1]
            defects = []
            for part, (centre, turned) in enumerate(((centre_real, -centre_imag), (centre_imag, centre_real))):
                beside = (
                    north_ref[...] * pltpu.roll(centre, rows - 1, 0)
                    + south_ref[...] * pltpu.roll(centre, 1, 0)
                    + east_ref[...] * pltpu.roll(centre, lanes - 1, 1)
                    + west_ref[...] * pltpu.roll(centre, 1, 1)
                )
                applied = diag_ref[...] * centre - beside + squeeze_number * turned
                defects.append(resid_ref[pair_index, part] - applied)
            real_diag = real_ref[...]
            step_scale = scale_ref[...]
            update_real = real_diag * defects[0] + squeeze_number * defects[1]
            update_imag = real_diag * defects[1] - squeeze_number * defects[0]
            out_ref[pair_index, 0] = centre_real + step_scale * update_real
            out_ref[pair_index, 1] = centre_imag + step_scale * update_imag
        return carry

    lax.fori_loop(0, SWEEPS, sweep, 0)


def local_solve(residual, edge_set, diagonal, inside):
    real_diag = jnp.where(inside > 0, diagonal, 1.0)
    step_scale = relaxation * inside / (real_diag * real_diag + squeeze_number * squeeze_number)
    rows, cols = diagonal.shape
    lanes = -(-cols // 128) * 128
    row_ids = jnp.arange(rows)[:, None]
    col_ids = jnp.arange(cols)[None, :]
    north_edge, south_edge, east_edge, west_edge = edge_set
    fields = [
        north_edge * (row_ids < rows - 1),
        south_edge * (row_ids > 0),
        east_edge * (col_ids < cols - 1),
        west_edge * (col_ids > 0),
        diagonal,
        real_diag,
        step_scale,
    ]
    widen = lambda field: jnp.pad(field, [(0, 0)] * (field.ndim - 1) + [(0, lanes - cols)])
    vmem = pl.BlockSpec(memory_space=pltpu.VMEM)
    result = pl.pallas_call(
        sweep_kernel,
        out_shape=jax.ShapeDtypeStruct(residual.shape[:2] + (rows, lanes), jnp.float32),
        in_specs=[vmem] * 8,
        out_specs=vmem,
        interpret=INTERPRET,
    )(widen(residual), *[widen(field.astype(jnp.float32)) for field in fields])
    return result[..., :cols]


def complex_scale(alpha_real, alpha_imag, vectors):
    return jnp.stack(
        [
            alpha_real * vectors[..., 0] - alpha_imag * vectors[..., 1],
            alpha_real * vectors[..., 1] + alpha_imag * vectors[..., 0],
        ],
        axis=-1,
    )


def plate_columns(width, tile_cols):
    first_col = lax.axis_index("gy") * tile_cols - width
    col_ids = first_col + jnp.arange(tile_cols + 2 * width, dtype=jnp.int32)
    return ((col_ids >= 0) & (col_ids < tile_cols * lax.axis_size("gy"))).astype(jnp.float32)


def body(forcing, gap_cubed, hole_mask, coarse_bases, basis_counts):
    mode_count = forcing.shape[0]
    tile_rows, tile_cols = gap_cubed.shape
    basis_total = coarse_bases.shape[0]
    deep_width = MARGIN + 1
    wide_rows = tile_rows + 2 * MARGIN
    wide_cols = tile_cols + 2 * MARGIN
    vent_term = vent_gain * hole_mask.astype(jnp.float32) * gap_cubed
    start_stack = jnp.concatenate(
        [gap_cubed[None], vent_term[None], forcing.reshape(2 * mode_count, tile_rows, tile_cols)],
        axis=0,
    )
    grown_stack = padded_2(start_stack, (("gx", 1), ("gy", 2)), deep_width)
    grown_stack = grown_stack * plate_columns(deep_width, tile_cols)
    gap_deep = grown_stack[0]
    vent_wide = grown_stack[1, 1:-1, 1:-1]
    force_wide = grown_stack[2:, 1:-1, 1:-1].reshape(mode_count, 2, wide_rows, wide_cols)
    inside = jnp.broadcast_to(plate_columns(MARGIN, tile_cols)[None, :], (wide_rows, wide_cols))
    wide_edges = edge_terms(gap_deep)
    wide_diag = diagonal_of(wide_edges, vent_wide)
    owned_edges = edge_terms(gap_deep[MARGIN:-MARGIN, MARGIN:-MARGIN])
    owned_diag = diagonal_of(owned_edges, vent_term)
    unit_mask = plate_columns(1, tile_cols)
    active = (jnp.arange(basis_total, dtype=jnp.int32) < basis_counts[0, 0]).astype(jnp.float32)
    base_field = coarse_bases * active[:, None, None]
    flat_bases = base_field.reshape(basis_total, tile_rows * tile_cols)

    def restrict(pressure):
        flat_field = pressure.reshape(2 * mode_count, tile_rows * tile_cols)
        product = lax.dot_general(
            flat_bases,
            flat_field,
            (((1,), (1,)), ((), ())),
            precision=highest,
            preferred_element_type=jnp.float32,
        )
        return product.reshape(basis_total, mode_count, 2)

    def prolong(coarse):
        product = lax.dot_general(
            coarse.reshape(basis_total, 2 * mode_count),
            flat_bases,
            (((0,), (0,)), ((), ())),
            precision=highest,
            preferred_element_type=jnp.float32,
        )
        return product.reshape(mode_count, 2, tile_rows, tile_cols)

    def pair(left, right):
        return lax.dot_general(
            left, right, (((1,), (1,)), ((), ())), precision=highest, preferred_element_type=jnp.float32
        )

    gx_count = lax.axis_size("gx")
    gy_count = lax.axis_size("gy")
    gy_index = lax.axis_index("gy")
    north_edge, south_edge, east_edge, west_edge = owned_edges
    from_next_x = lax.ppermute(base_field[:, 0, :], "gx", [((i + 1) % gx_count, i) for i in range(gx_count)])
    from_prev_x = lax.ppermute(base_field[:, -1, :], "gx", [(i, (i + 1) % gx_count) for i in range(gx_count)])
    from_next_y = lax.ppermute(base_field[:, :, 0], "gy", [((i + 1) % gy_count, i) for i in range(gy_count)])
    from_prev_y = lax.ppermute(base_field[:, :, -1], "gy", [(i, (i + 1) % gy_count) for i in range(gy_count)])
    has_next_y = (gy_index < gy_count - 1).astype(jnp.float32)
    has_prev_y = (gy_index > 0).astype(jnp.float32)
    base_padded = jnp.pad(base_field, ((0, 0), (1, 1), (1, 1)))
    base_image = owned_diag * base_field - (
        north_edge * base_padded[:, 2:, 1:-1]
        + south_edge * base_padded[:, :-2, 1:-1]
        + east_edge * base_padded[:, 1:-1, 2:]
        + west_edge * base_padded[:, 1:-1, :-2]
    )
    self_block = pair(flat_bases, base_image.reshape(basis_total, tile_rows * tile_cols))
    gram_block = pair(flat_bases, flat_bases)
    next_x_block = -pair(base_field[:, -1, :] * north_edge[-1], from_next_x)
    prev_x_block = -pair(base_field[:, 0, :] * south_edge[0], from_prev_x)
    next_y_block = -pair(base_field[:, :, -1] * east_edge[:, -1], from_next_y) * has_next_y
    prev_y_block = -pair(base_field[:, :, 0] * west_edge[:, 0], from_prev_y) * has_prev_y
    block_set = jnp.stack(
        [self_block, next_x_block, prev_x_block, next_y_block, prev_y_block, squeeze_number * gram_block]
    )
    tile_total = gx_count * gy_count
    gathered_blocks = lax.all_gather(block_set.reshape(1, -1), ("gx", "gy"), axis=0, tiled=True)
    all_blocks = gathered_blocks.T.reshape(block_set.shape + (tile_total,))

    def coarse_image(search):
        halves = search.reshape(basis_total, mode_count, 2, tile_total)
        turned = jnp.stack([-halves[:, :, 1], halves[:, :, 0]], axis=2).reshape(search.shape)
        shifted = (
            search,
            jnp.roll(search, -gy_count, axis=-1),
            jnp.roll(search, gy_count, axis=-1),
            jnp.roll(search, -1, axis=-1),
            jnp.roll(search, 1, axis=-1),
            turned,
        )
        total = None
        for block, vectors in zip(all_blocks, shifted):
            term = jnp.sum(block[:, :, None, :] * vectors[None, :, :, :], axis=1)
            total = term if total is None else total + term
        return total

    gx_index = lax.axis_index("gx")
    tile_index = gx_index * gy_count + gy_index
    solution = jnp.zeros_like(forcing)
    residual_wide = force_wide
    for outer_step in range(ITERS):
        if outer_step > 0:
            solution_deep = padded_2(solution, (("gx", 2), ("gy", 3)), deep_width) * plate_columns(deep_width, tile_cols)
            residual_wide = force_wide - apply_operator(solution_deep, wide_edges, wide_diag)
            residual_wide = residual_wide * plate_columns(MARGIN, tile_cols)
        residual = residual_wide[:, :, MARGIN:-MARGIN, MARGIN:-MARGIN]
        local_part = local_solve(residual_wide, wide_edges, wide_diag, inside)[
            :, :, MARGIN:-MARGIN, MARGIN:-MARGIN
        ]
        gathered = tree_gather(restrict(residual).reshape(-1), ("gy", "gx"))
        search = gathered.reshape(tile_total, -1).T.reshape(basis_total, 2 * mode_count, tile_total)
        coarse = jnp.zeros_like(search)
        for coarse_step in range(CSTEPS):
            images = coarse_image(search)
            image_halves = images.reshape(basis_total, mode_count, 2, tile_total)
            search_halves = search.reshape(basis_total, mode_count, 2, tile_total)
            num_real = jnp.sum(
                image_halves[:, :, 0] * search_halves[:, :, 0] + image_halves[:, :, 1] * search_halves[:, :, 1],
                axis=(0, 2),
            )
            num_imag = jnp.sum(
                image_halves[:, :, 0] * search_halves[:, :, 1] - image_halves[:, :, 1] * search_halves[:, :, 0],
                axis=(0, 2),
            )
            squares = jnp.sum(image_halves * image_halves, axis=(0, 2, 3))
            denominator = squares + guard_value
            alpha_real = (num_real / denominator)[None, :, None]
            alpha_imag = (num_imag / denominator)[None, :, None]
            coarse_halves = coarse.reshape(search_halves.shape)
            coarse = jnp.stack(
                [
                    coarse_halves[:, :, 0] + alpha_real * search_halves[:, :, 0] - alpha_imag * search_halves[:, :, 1],
                    coarse_halves[:, :, 1] + alpha_real * search_halves[:, :, 1] + alpha_imag * search_halves[:, :, 0],
                ],
                axis=2,
            ).reshape(search.shape)
            search = jnp.stack(
                [
                    search_halves[:, :, 0] - (alpha_real * image_halves[:, :, 0] - alpha_imag * image_halves[:, :, 1]),
                    search_halves[:, :, 1] - (alpha_real * image_halves[:, :, 1] + alpha_imag * image_halves[:, :, 0]),
                ],
                axis=2,
            ).reshape(search.shape)
        own_coarse = lax.dynamic_index_in_dim(coarse, tile_index, axis=2, keepdims=False)
        solution = solution + local_part + prolong(own_coarse)
    return solution


def solution(mesh):
    placed = (
        P(None, None, "gx", "gy"),
        P("gx", "gy"),
        P("gx", "gy"),
        P(None, "gx", "gy"),
        P("gx", "gy"),
    )
    return jax.shard_map(
        body, mesh=mesh, in_specs=placed, out_specs=P(None, None, "gx", "gy"), check_vma=False
    )
```

```python
import jax
import jax.numpy as jnp
from jax import lax
from jax.experimental import pallas as pl
from jax.experimental.pallas import tpu as pltpu
from jax.sharding import PartitionSpec as P

MARGIN = 16
SWEEPS = 20
CSTEPS = 7
ITERS = 2


squeeze_number = 0.2
vent_gain = 4.0
relaxation = 0.8
guard_value = 1e-12
highest = lax.Precision.HIGHEST


def padded_2(cells, sides, width):
    for axis, dim in sides:
        count = lax.axis_size(axis)
        head = lax.slice_in_dim(cells, 0, width, axis=dim)
        tail = lax.slice_in_dim(cells, cells.shape[dim] - width, cells.shape[dim], axis=dim)
        cells = jnp.concatenate(
            [
                lax.ppermute(tail, axis, [(i, (i + 1) % count) for i in range(count)]),
                cells,
                lax.ppermute(head, axis, [((i + 1) % count, i) for i in range(count)]),
            ],
            axis=dim,
        )
    return cells


def tree_sum(values, axes):
    for axis in axes:
        count = lax.axis_size(axis)
        if count & (count - 1):
            values = lax.psum(values, axis)
            continue
        stride = 1
        while stride < count:
            values = values + lax.ppermute(values, axis, [(i, i ^ stride) for i in range(count)])
            stride *= 2
    return values


def tree_gather(values, axes):
    for axis in axes:
        count = lax.axis_size(axis)
        if count & (count - 1):
            values = lax.all_gather(values, axis)
            continue
        index = lax.axis_index(axis)
        values = values[None]
        stride = 1
        while stride < count:
            other = lax.ppermute(values, axis, [(i, i ^ stride) for i in range(count)])
            upper = (index // stride) % 2 == 1
            values = jnp.where(upper, jnp.concatenate([other, values]), jnp.concatenate([values, other]))
            stride *= 2
    return values


def edge_terms(gap_padded):
    centre = gap_padded[1:-1, 1:-1]
    north_edge = 0.5 * (centre + gap_padded[2:, 1:-1])
    south_edge = 0.5 * (centre + gap_padded[:-2, 1:-1])
    east_edge = 0.5 * (centre + gap_padded[1:-1, 2:])
    west_edge = 0.5 * (centre + gap_padded[1:-1, :-2])
    return (north_edge, south_edge, east_edge, west_edge)


def diagonal_of(edge_set, vent_term):
    return edge_set[0] + edge_set[1] + edge_set[2] + edge_set[3] + vent_term


def apply_operator(padded, edge_set, diagonal):
    north_edge, south_edge, east_edge, west_edge = edge_set
    centre = padded[:, :, 1:-1, 1:-1]
    beside_all = (
        north_edge * padded[:, :, 2:, 1:-1]
        + south_edge * padded[:, :, :-2, 1:-1]
        + east_edge * padded[:, :, 1:-1, 2:]
        + west_edge * padded[:, :, 1:-1, :-2]
    )
    turned = jnp.stack([-centre[:, 1], centre[:, 0]], axis=1)
    return diagonal * centre - beside_all + squeeze_number * turned


INTERPRET = False


def sweep_kernel(resid_ref, north_ref, south_ref, east_ref, west_ref, diag_ref, real_ref, scale_ref, out_ref):
    pairs, _, rows, lanes = out_ref.shape
    out_ref[...] = jnp.zeros(out_ref.shape, jnp.float32)

    def sweep(sweep_index, carry):
        for pair_index in range(pairs):
            centre_real = out_ref[pair_index, 0]
            centre_imag = out_ref[pair_index, 1]
            defects = []
            for part, (centre, turned) in enumerate(((centre_real, -centre_imag), (centre_imag, centre_real))):
                beside = (
                    north_ref[...] * pltpu.roll(centre, rows - 1, 0)
                    + south_ref[...] * pltpu.roll(centre, 1, 0)
                    + east_ref[...] * pltpu.roll(centre, lanes - 1, 1)
                    + west_ref[...] * pltpu.roll(centre, 1, 1)
                )
                applied = diag_ref[...] * centre - beside + squeeze_number * turned
                defects.append(resid_ref[pair_index, part] - applied)
            real_diag = real_ref[...]
            step_scale = scale_ref[...]
            update_real = real_diag * defects[0] + squeeze_number * defects[1]
            update_imag = real_diag * defects[1] - squeeze_number * defects[0]
            out_ref[pair_index, 0] = centre_real + step_scale * update_real
            out_ref[pair_index, 1] = centre_imag + step_scale * update_imag
        return carry

    lax.fori_loop(0, SWEEPS, sweep, 0)


def local_solve(residual, edge_set, diagonal, inside):
    real_diag = jnp.where(inside > 0, diagonal, 1.0)
    step_scale = relaxation * inside / (real_diag * real_diag + squeeze_number * squeeze_number)
    rows, cols = diagonal.shape
    lanes = -(-cols // 128) * 128
    row_ids = jnp.arange(rows)[:, None]
    col_ids = jnp.arange(cols)[None, :]
    north_edge, south_edge, east_edge, west_edge = edge_set
    fields = [
        north_edge * (row_ids < rows - 1),
        south_edge * (row_ids > 0),
        east_edge * (col_ids < cols - 1),
        west_edge * (col_ids > 0),
        diagonal,
        real_diag,
        step_scale,
    ]
    widen = lambda field: jnp.pad(field, [(0, 0)] * (field.ndim - 1) + [(0, lanes - cols)])
    vmem = pl.BlockSpec(memory_space=pltpu.VMEM)
    result = pl.pallas_call(
        sweep_kernel,
        out_shape=jax.ShapeDtypeStruct(residual.shape[:2] + (rows, lanes), jnp.float32),
        in_specs=[vmem] * 8,
        out_specs=vmem,
        interpret=INTERPRET,
    )(widen(residual), *[widen(field.astype(jnp.float32)) for field in fields])
    return result[..., :cols]


def complex_scale(alpha_real, alpha_imag, vectors):
    return jnp.stack(
        [
            alpha_real * vectors[..., 0] - alpha_imag * vectors[..., 1],
            alpha_real * vectors[..., 1] + alpha_imag * vectors[..., 0],
        ],
        axis=-1,
    )


def plate_columns(width, tile_cols):
    first_col = lax.axis_index("gy") * tile_cols - width
    col_ids = first_col + jnp.arange(tile_cols + 2 * width, dtype=jnp.int32)
    return ((col_ids >= 0) & (col_ids < tile_cols * lax.axis_size("gy"))).astype(jnp.float32)


def body(forcing, gap_cubed, hole_mask, coarse_bases, basis_counts):
    mode_count = forcing.shape[0]
    tile_rows, tile_cols = gap_cubed.shape
    basis_total = coarse_bases.shape[0]
    deep_width = MARGIN + 1
    wide_rows = tile_rows + 2 * MARGIN
    wide_cols = tile_cols + 2 * MARGIN
    vent_term = vent_gain * hole_mask.astype(jnp.float32) * gap_cubed
    start_stack = jnp.concatenate(
        [gap_cubed[None], vent_term[None], forcing.reshape(2 * mode_count, tile_rows, tile_cols)],
        axis=0,
    )
    grown_stack = padded_2(start_stack, (("gx", 1), ("gy", 2)), deep_width)
    grown_stack = grown_stack * plate_columns(deep_width, tile_cols)
    gap_deep = grown_stack[0]
    vent_wide = grown_stack[1, 1:-1, 1:-1]
    force_wide = grown_stack[2:, 1:-1, 1:-1].reshape(mode_count, 2, wide_rows, wide_cols)
    inside = jnp.broadcast_to(plate_columns(MARGIN, tile_cols)[None, :], (wide_rows, wide_cols))
    wide_edges = edge_terms(gap_deep)
    wide_diag = diagonal_of(wide_edges, vent_wide)
    owned_edges = edge_terms(gap_deep[MARGIN:-MARGIN, MARGIN:-MARGIN])
    owned_diag = diagonal_of(owned_edges, vent_term)
    unit_mask = plate_columns(1, tile_cols)
    active = (jnp.arange(basis_total, dtype=jnp.int32) < basis_counts[0, 0]).astype(jnp.float32)
    base_field = coarse_bases * active[:, None, None]
    flat_bases = base_field.reshape(basis_total, tile_rows * tile_cols)

    def restrict(pressure):
        flat_field = pressure.reshape(2 * mode_count, tile_rows * tile_cols)
        product = lax.dot_general(
            flat_bases,
            flat_field,
            (((1,), (1,)), ((), ())),
            precision=highest,
            preferred_element_type=jnp.float32,
        )
        return product.reshape(basis_total, mode_count, 2)

    def prolong(coarse):
        product = lax.dot_general(
            coarse.reshape(basis_total, 2 * mode_count),
            flat_bases,
            (((0,), (0,)), ((), ())),
            precision=highest,
            preferred_element_type=jnp.float32,
        )
        return product.reshape(mode_count, 2, tile_rows, tile_cols)

    def pair(left, right):
        return lax.dot_general(
            left, right, (((1,), (1,)), ((), ())), precision=highest, preferred_element_type=jnp.float32
        )

    gx_count = lax.axis_size("gx")
    gy_count = lax.axis_size("gy")
    gy_index = lax.axis_index("gy")
    north_edge, south_edge, east_edge, west_edge = owned_edges
    from_next_x = lax.ppermute(base_field[:, 0, :], "gx", [((i + 1) % gx_count, i) for i in range(gx_count)])
    from_prev_x = lax.ppermute(base_field[:, -1, :], "gx", [(i, (i + 1) % gx_count) for i in range(gx_count)])
    from_next_y = lax.ppermute(base_field[:, :, 0], "gy", [((i + 1) % gy_count, i) for i in range(gy_count)])
    from_prev_y = lax.ppermute(base_field[:, :, -1], "gy", [(i, (i + 1) % gy_count) for i in range(gy_count)])
    has_next_y = (gy_index < gy_count - 1).astype(jnp.float32)
    has_prev_y = (gy_index > 0).astype(jnp.float32)
    base_padded = jnp.pad(base_field, ((0, 0), (1, 1), (1, 1)))
    base_image = owned_diag * base_field - (
        north_edge * base_padded[:, 2:, 1:-1]
        + south_edge * base_padded[:, :-2, 1:-1]
        + east_edge * base_padded[:, 1:-1, 2:]
        + west_edge * base_padded[:, 1:-1, :-2]
    )
    self_block = pair(flat_bases, base_image.reshape(basis_total, tile_rows * tile_cols))
    gram_block = pair(flat_bases, flat_bases)
    next_x_block = -pair(base_field[:, -1, :] * north_edge[-1], from_next_x)
    prev_x_block = -pair(base_field[:, 0, :] * south_edge[0], from_prev_x)
    next_y_block = -pair(base_field[:, :, -1] * east_edge[:, -1], from_next_y) * has_next_y
    prev_y_block = -pair(base_field[:, :, 0] * west_edge[:, 0], from_prev_y) * has_prev_y
    block_set = jnp.stack(
        [self_block.T, next_x_block.T, prev_x_block.T, next_y_block.T, prev_y_block.T, squeeze_number * gram_block.T]
    )
    tile_total = gx_count * gy_count
    gathered_blocks = lax.all_gather(block_set.reshape(1, -1), ("gx", "gy"), axis=0, tiled=True)
    all_blocks = gathered_blocks.T.reshape(block_set.shape + (tile_total,))

    def coarse_image(search):
        halves = search.reshape(mode_count, 2, basis_total, tile_total)
        turned = jnp.stack([-halves[:, 1], halves[:, 0]], axis=1).reshape(search.shape)
        shifted = (
            search,
            jnp.roll(search, -gy_count, axis=-1),
            jnp.roll(search, gy_count, axis=-1),
            jnp.roll(search, -1, axis=-1),
            jnp.roll(search, 1, axis=-1),
            turned,
        )
        total = None
        for block, vectors in zip(all_blocks, shifted):
            term = jnp.sum(block[None, :, :, :] * vectors[:, :, None, :], axis=1)
            total = term if total is None else total + term
        return total

    gx_index = lax.axis_index("gx")
    tile_index = gx_index * gy_count + gy_index
    solution = jnp.zeros_like(forcing)
    residual_wide = force_wide
    for outer_step in range(ITERS):
        if outer_step > 0:
            solution_deep = padded_2(solution, (("gx", 2), ("gy", 3)), deep_width) * plate_columns(deep_width, tile_cols)
            residual_wide = force_wide - apply_operator(solution_deep, wide_edges, wide_diag)
            residual_wide = residual_wide * plate_columns(MARGIN, tile_cols)
        residual = residual_wide[:, :, MARGIN:-MARGIN, MARGIN:-MARGIN]
        local_part = local_solve(residual_wide, wide_edges, wide_diag, inside)[
            :, :, MARGIN:-MARGIN, MARGIN:-MARGIN
        ]
        gathered = tree_gather(restrict(residual).reshape(-1), ("gy", "gx"))
        search = gathered.reshape(tile_total, basis_total, 2 * mode_count).transpose(2, 1, 0)
        coarse = jnp.zeros_like(search)
        for coarse_step in range(CSTEPS):
            images = coarse_image(search)
            image_halves = images.reshape(mode_count, 2, basis_total, tile_total)
            search_halves = search.reshape(mode_count, 2, basis_total, tile_total)
            num_real = jnp.sum(
                image_halves[:, 0] * search_halves[:, 0] + image_halves[:, 1] * search_halves[:, 1],
                axis=(1, 2),
            )
            num_imag = jnp.sum(
                image_halves[:, 0] * search_halves[:, 1] - image_halves[:, 1] * search_halves[:, 0],
                axis=(1, 2),
            )
            squares = jnp.sum(image_halves * image_halves, axis=(1, 2, 3))
            denominator = squares + guard_value
            alpha_real = (num_real / denominator)[:, None, None]
            alpha_imag = (num_imag / denominator)[:, None, None]
            coarse_halves = coarse.reshape(search_halves.shape)
            coarse = jnp.stack(
                [
                    coarse_halves[:, 0] + alpha_real * search_halves[:, 0] - alpha_imag * search_halves[:, 1],
                    coarse_halves[:, 1] + alpha_real * search_halves[:, 1] + alpha_imag * search_halves[:, 0],
                ],
                axis=1,
            ).reshape(search.shape)
            search = jnp.stack(
                [
                    search_halves[:, 0] - (alpha_real * image_halves[:, 0] - alpha_imag * image_halves[:, 1]),
                    search_halves[:, 1] - (alpha_real * image_halves[:, 1] + alpha_imag * image_halves[:, 0]),
                ],
                axis=1,
            ).reshape(search.shape)
        own_coarse = lax.dynamic_index_in_dim(coarse, tile_index, axis=2, keepdims=False).T
        solution = solution + local_part + prolong(own_coarse)
    return solution


def solution(mesh):
    placed = (
        P(None, None, "gx", "gy"),
        P("gx", "gy"),
        P("gx", "gy"),
        P(None, "gx", "gy"),
        P("gx", "gy"),
    )
    return jax.shard_map(
        body, mesh=mesh, in_specs=placed, out_specs=P(None, None, "gx", "gy"), check_vma=False
    )
```

```python
import jax
import jax.numpy as jnp
from jax import lax
from jax.experimental import pallas as pl
from jax.experimental.pallas import tpu as pltpu
from jax.sharding import PartitionSpec as P

MARGIN = 16
SWEEPS = 20
CSTEPS = 7
ITERS = 2


squeeze_number = 0.2
vent_gain = 4.0
relaxation = 0.8
guard_value = 1e-12
highest = lax.Precision.HIGHEST


def padded_2(cells, sides, width):
    for axis, dim in sides:
        count = lax.axis_size(axis)
        head = lax.slice_in_dim(cells, 0, width, axis=dim)
        tail = lax.slice_in_dim(cells, cells.shape[dim] - width, cells.shape[dim], axis=dim)
        cells = jnp.concatenate(
            [
                lax.ppermute(tail, axis, [(i, (i + 1) % count) for i in range(count)]),
                cells,
                lax.ppermute(head, axis, [((i + 1) % count, i) for i in range(count)]),
            ],
            axis=dim,
        )
    return cells


def tree_sum(values, axes):
    for axis in axes:
        count = lax.axis_size(axis)
        if count & (count - 1):
            values = lax.psum(values, axis)
            continue
        stride = 1
        while stride < count:
            values = values + lax.ppermute(values, axis, [(i, i ^ stride) for i in range(count)])
            stride *= 2
    return values


def tree_gather(values, axes):
    for axis in axes:
        count = lax.axis_size(axis)
        if count & (count - 1):
            values = lax.all_gather(values, axis)
            continue
        index = lax.axis_index(axis)
        values = values[None]
        stride = 1
        while stride < count:
            other = lax.ppermute(values, axis, [(i, i ^ stride) for i in range(count)])
            upper = (index // stride) % 2 == 1
            values = jnp.where(upper, jnp.concatenate([other, values]), jnp.concatenate([values, other]))
            stride *= 2
    return values


def edge_terms(gap_padded):
    centre = gap_padded[1:-1, 1:-1]
    north_edge = 0.5 * (centre + gap_padded[2:, 1:-1])
    south_edge = 0.5 * (centre + gap_padded[:-2, 1:-1])
    east_edge = 0.5 * (centre + gap_padded[1:-1, 2:])
    west_edge = 0.5 * (centre + gap_padded[1:-1, :-2])
    return (north_edge, south_edge, east_edge, west_edge)


def diagonal_of(edge_set, vent_term):
    return edge_set[0] + edge_set[1] + edge_set[2] + edge_set[3] + vent_term


def apply_operator(padded, edge_set, diagonal):
    north_edge, south_edge, east_edge, west_edge = edge_set
    centre = padded[:, :, 1:-1, 1:-1]
    beside_all = (
        north_edge * padded[:, :, 2:, 1:-1]
        + south_edge * padded[:, :, :-2, 1:-1]
        + east_edge * padded[:, :, 1:-1, 2:]
        + west_edge * padded[:, :, 1:-1, :-2]
    )
    turned = jnp.stack([-centre[:, 1], centre[:, 0]], axis=1)
    return diagonal * centre - beside_all + squeeze_number * turned


INTERPRET = False


def sweep_kernel(resid_ref, north_ref, south_ref, east_ref, west_ref, diag_ref, real_ref, scale_ref, out_ref):
    pairs, _, rows, lanes = out_ref.shape
    out_ref[...] = jnp.zeros(out_ref.shape, jnp.float32)

    def sweep(sweep_index, carry):
        for pair_index in range(pairs):
            centre_real = out_ref[pair_index, 0]
            centre_imag = out_ref[pair_index, 1]
            defects = []
            for part, (centre, turned) in enumerate(((centre_real, -centre_imag), (centre_imag, centre_real))):
                beside = (
                    north_ref[...] * pltpu.roll(centre, rows - 1, 0)
                    + south_ref[...] * pltpu.roll(centre, 1, 0)
                    + east_ref[...] * pltpu.roll(centre, lanes - 1, 1)
                    + west_ref[...] * pltpu.roll(centre, 1, 1)
                )
                applied = diag_ref[...] * centre - beside + squeeze_number * turned
                defects.append(resid_ref[pair_index, part] - applied)
            real_diag = real_ref[...]
            step_scale = scale_ref[...]
            update_real = real_diag * defects[0] + squeeze_number * defects[1]
            update_imag = real_diag * defects[1] - squeeze_number * defects[0]
            out_ref[pair_index, 0] = centre_real + step_scale * update_real
            out_ref[pair_index, 1] = centre_imag + step_scale * update_imag
        return carry

    lax.fori_loop(0, SWEEPS, sweep, 0)


def local_solve(residual, edge_set, diagonal, inside):
    real_diag = jnp.where(inside > 0, diagonal, 1.0)
    step_scale = relaxation * inside / (real_diag * real_diag + squeeze_number * squeeze_number)
    rows, cols = diagonal.shape
    lanes = -(-cols // 128) * 128
    row_ids = jnp.arange(rows)[:, None]
    col_ids = jnp.arange(cols)[None, :]
    north_edge, south_edge, east_edge, west_edge = edge_set
    fields = [
        north_edge * (row_ids < rows - 1),
        south_edge * (row_ids > 0),
        east_edge * (col_ids < cols - 1),
        west_edge * (col_ids > 0),
        diagonal,
        real_diag,
        step_scale,
    ]
    widen = lambda field: jnp.pad(field, [(0, 0)] * (field.ndim - 1) + [(0, lanes - cols)])
    vmem = pl.BlockSpec(memory_space=pltpu.VMEM)
    result = pl.pallas_call(
        sweep_kernel,
        out_shape=jax.ShapeDtypeStruct(residual.shape[:2] + (rows, lanes), jnp.float32),
        in_specs=[vmem] * 8,
        out_specs=vmem,
        interpret=INTERPRET,
    )(widen(residual), *[widen(field.astype(jnp.float32)) for field in fields])
    return result[..., :cols]


def complex_scale(alpha_real, alpha_imag, vectors):
    return jnp.stack(
        [
            alpha_real * vectors[..., 0] - alpha_imag * vectors[..., 1],
            alpha_real * vectors[..., 1] + alpha_imag * vectors[..., 0],
        ],
        axis=-1,
    )


def plate_columns(width, tile_cols):
    first_col = lax.axis_index("gy") * tile_cols - width
    col_ids = first_col + jnp.arange(tile_cols + 2 * width, dtype=jnp.int32)
    return ((col_ids >= 0) & (col_ids < tile_cols * lax.axis_size("gy"))).astype(jnp.float32)


def body(forcing, gap_cubed, hole_mask, coarse_bases, basis_counts):
    mode_count = forcing.shape[0]
    tile_rows, tile_cols = gap_cubed.shape
    basis_total = coarse_bases.shape[0]
    deep_width = MARGIN + 1
    wide_rows = tile_rows + 2 * MARGIN
    wide_cols = tile_cols + 2 * MARGIN
    vent_term = vent_gain * hole_mask.astype(jnp.float32) * gap_cubed
    start_stack = jnp.concatenate(
        [gap_cubed[None], vent_term[None], forcing.reshape(2 * mode_count, tile_rows, tile_cols)],
        axis=0,
    )
    grown_stack = padded_2(start_stack, (("gx", 1), ("gy", 2)), deep_width)
    grown_stack = grown_stack * plate_columns(deep_width, tile_cols)
    gap_deep = grown_stack[0]
    vent_wide = grown_stack[1, 1:-1, 1:-1]
    force_wide = grown_stack[2:, 1:-1, 1:-1].reshape(mode_count, 2, wide_rows, wide_cols)
    inside = jnp.broadcast_to(plate_columns(MARGIN, tile_cols)[None, :], (wide_rows, wide_cols))
    wide_edges = edge_terms(gap_deep)
    wide_diag = diagonal_of(wide_edges, vent_wide)
    owned_edges = edge_terms(gap_deep[MARGIN:-MARGIN, MARGIN:-MARGIN])
    owned_diag = diagonal_of(owned_edges, vent_term)
    unit_mask = plate_columns(1, tile_cols)
    active = (jnp.arange(basis_total, dtype=jnp.int32) < basis_counts[0, 0]).astype(jnp.float32)
    base_field = coarse_bases * active[:, None, None]
    flat_bases = base_field.reshape(basis_total, tile_rows * tile_cols)

    def restrict(pressure):
        flat_field = pressure.reshape(2 * mode_count, tile_rows * tile_cols)
        product = lax.dot_general(
            flat_bases,
            flat_field,
            (((1,), (1,)), ((), ())),
            precision=highest,
            preferred_element_type=jnp.float32,
        )
        return product.reshape(basis_total, mode_count, 2)

    def prolong(coarse):
        product = lax.dot_general(
            coarse.reshape(basis_total, 2 * mode_count),
            flat_bases,
            (((0,), (0,)), ((), ())),
            precision=highest,
            preferred_element_type=jnp.float32,
        )
        return product.reshape(mode_count, 2, tile_rows, tile_cols)

    def pair(left, right):
        return lax.dot_general(
            left, right, (((1,), (1,)), ((), ())), precision=highest, preferred_element_type=jnp.float32
        )

    gx_count = lax.axis_size("gx")
    gy_count = lax.axis_size("gy")
    gy_index = lax.axis_index("gy")
    north_edge, south_edge, east_edge, west_edge = owned_edges
    from_next_x = lax.ppermute(base_field[:, 0, :], "gx", [((i + 1) % gx_count, i) for i in range(gx_count)])
    from_prev_x = lax.ppermute(base_field[:, -1, :], "gx", [(i, (i + 1) % gx_count) for i in range(gx_count)])
    from_next_y = lax.ppermute(base_field[:, :, 0], "gy", [((i + 1) % gy_count, i) for i in range(gy_count)])
    from_prev_y = lax.ppermute(base_field[:, :, -1], "gy", [(i, (i + 1) % gy_count) for i in range(gy_count)])
    has_next_y = (gy_index < gy_count - 1).astype(jnp.float32)
    has_prev_y = (gy_index > 0).astype(jnp.float32)
    base_padded = jnp.pad(base_field, ((0, 0), (1, 1), (1, 1)))
    base_image = owned_diag * base_field - (
        north_edge * base_padded[:, 2:, 1:-1]
        + south_edge * base_padded[:, :-2, 1:-1]
        + east_edge * base_padded[:, 1:-1, 2:]
        + west_edge * base_padded[:, 1:-1, :-2]
    )
    self_block = pair(flat_bases, base_image.reshape(basis_total, tile_rows * tile_cols))
    gram_block = pair(flat_bases, flat_bases)
    next_x_block = -pair(base_field[:, -1, :] * north_edge[-1], from_next_x)
    prev_x_block = -pair(base_field[:, 0, :] * south_edge[0], from_prev_x)
    next_y_block = -pair(base_field[:, :, -1] * east_edge[:, -1], from_next_y) * has_next_y
    prev_y_block = -pair(base_field[:, :, 0] * west_edge[:, 0], from_prev_y) * has_prev_y
    block_set = jnp.stack(
        [self_block.T, next_x_block.T, prev_x_block.T, next_y_block.T, prev_y_block.T, squeeze_number * gram_block.T]
    )
    tile_total = gx_count * gy_count
    gathered_blocks = lax.all_gather(block_set.reshape(1, -1), ("gx", "gy"), axis=0, tiled=True)
    all_blocks = gathered_blocks.T.reshape(block_set.shape + (tile_total,))

    tile_ids = jnp.arange(tile_total)
    movers = [
        (tile_ids[:, None] == (tile_ids[None, :] + offset) % tile_total).astype(jnp.float32)
        for offset in (gy_count, -gy_count, 1, -1)
    ]

    def coarse_image(search):
        halves = search.reshape(mode_count, 2, basis_total, tile_total)
        turned = jnp.stack([-halves[:, 1], halves[:, 0]], axis=1).reshape(search.shape)
        flat = search.reshape(-1, tile_total)
        moved = [
            lax.dot_general(
                flat, mover, (((1,), (0,)), ((), ())), precision=highest, preferred_element_type=jnp.float32
            ).reshape(search.shape)
            for mover in movers
        ]
        shifted = (search, *moved, turned)
        total = None
        for block, vectors in zip(all_blocks, shifted):
            term = jnp.sum(block[None, :, :, :] * vectors[:, :, None, :], axis=1)
            total = term if total is None else total + term
        return total

    gx_index = lax.axis_index("gx")
    tile_index = gx_index * gy_count + gy_index
    solution = jnp.zeros_like(forcing)
    residual_wide = force_wide
    for outer_step in range(ITERS):
        if outer_step > 0:
            solution_deep = padded_2(solution, (("gx", 2), ("gy", 3)), deep_width) * plate_columns(deep_width, tile_cols)
            residual_wide = force_wide - apply_operator(solution_deep, wide_edges, wide_diag)
            residual_wide = residual_wide * plate_columns(MARGIN, tile_cols)
        residual = residual_wide[:, :, MARGIN:-MARGIN, MARGIN:-MARGIN]
        local_part = local_solve(residual_wide, wide_edges, wide_diag, inside)[
            :, :, MARGIN:-MARGIN, MARGIN:-MARGIN
        ]
        gathered = tree_gather(restrict(residual).reshape(-1), ("gy", "gx"))
        search = gathered.reshape(tile_total, basis_total, 2 * mode_count).transpose(2, 1, 0)
        coarse = jnp.zeros_like(search)
        for coarse_step in range(CSTEPS):
            images = coarse_image(search)
            image_halves = images.reshape(mode_count, 2, basis_total, tile_total)
            search_halves = search.reshape(mode_count, 2, basis_total, tile_total)
            num_real = jnp.sum(
                image_halves[:, 0] * search_halves[:, 0] + image_halves[:, 1] * search_halves[:, 1],
                axis=(1, 2),
            )
            num_imag = jnp.sum(
                image_halves[:, 0] * search_halves[:, 1] - image_halves[:, 1] * search_halves[:, 0],
                axis=(1, 2),
            )
            squares = jnp.sum(image_halves * image_halves, axis=(1, 2, 3))
            denominator = squares + guard_value
            alpha_real = (num_real / denominator)[:, None, None]
            alpha_imag = (num_imag / denominator)[:, None, None]
            coarse_halves = coarse.reshape(search_halves.shape)
            coarse = jnp.stack(
                [
                    coarse_halves[:, 0] + alpha_real * search_halves[:, 0] - alpha_imag * search_halves[:, 1],
                    coarse_halves[:, 1] + alpha_real * search_halves[:, 1] + alpha_imag * search_halves[:, 0],
                ],
                axis=1,
            ).reshape(search.shape)
            search = jnp.stack(
                [
                    search_halves[:, 0] - (alpha_real * image_halves[:, 0] - alpha_imag * image_halves[:, 1]),
                    search_halves[:, 1] - (alpha_real * image_halves[:, 1] + alpha_imag * image_halves[:, 0]),
                ],
                axis=1,
            ).reshape(search.shape)
        own_coarse = lax.dynamic_index_in_dim(coarse, tile_index, axis=2, keepdims=False).T
        solution = solution + local_part + prolong(own_coarse)
    return solution


def solution(mesh):
    placed = (
        P(None, None, "gx", "gy"),
        P("gx", "gy"),
        P("gx", "gy"),
        P(None, "gx", "gy"),
        P("gx", "gy"),
    )
    return jax.shard_map(
        body, mesh=mesh, in_specs=placed, out_specs=P(None, None, "gx", "gy"), check_vma=False
    )
```

```python
import jax
import jax.numpy as jnp
from jax import lax
from jax.experimental import pallas as pl
from jax.experimental.pallas import tpu as pltpu
from jax.sharding import PartitionSpec as P

MARGIN = 16
SWEEPS = 20
CSTEPS = 7
ITERS = 2


squeeze_number = 0.2
vent_gain = 4.0
relaxation = 0.8
guard_value = 1e-12
highest = lax.Precision.HIGHEST


def padded_2(cells, sides, width):
    for axis, dim in sides:
        count = lax.axis_size(axis)
        head = lax.slice_in_dim(cells, 0, width, axis=dim)
        tail = lax.slice_in_dim(cells, cells.shape[dim] - width, cells.shape[dim], axis=dim)
        cells = jnp.concatenate(
            [
                lax.ppermute(tail, axis, [(i, (i + 1) % count) for i in range(count)]),
                cells,
                lax.ppermute(head, axis, [((i + 1) % count, i) for i in range(count)]),
            ],
            axis=dim,
        )
    return cells


def tree_sum(values, axes):
    for axis in axes:
        count = lax.axis_size(axis)
        if count & (count - 1):
            values = lax.psum(values, axis)
            continue
        stride = 1
        while stride < count:
            values = values + lax.ppermute(values, axis, [(i, i ^ stride) for i in range(count)])
            stride *= 2
    return values


def tree_gather(values, axes):
    for axis in axes:
        count = lax.axis_size(axis)
        if count & (count - 1):
            values = lax.all_gather(values, axis)
            continue
        index = lax.axis_index(axis)
        values = values[None]
        stride = 1
        while stride < count:
            other = lax.ppermute(values, axis, [(i, i ^ stride) for i in range(count)])
            upper = (index // stride) % 2 == 1
            values = jnp.where(upper, jnp.concatenate([other, values]), jnp.concatenate([values, other]))
            stride *= 2
    return values


def edge_terms(gap_padded):
    centre = gap_padded[1:-1, 1:-1]
    north_edge = 0.5 * (centre + gap_padded[2:, 1:-1])
    south_edge = 0.5 * (centre + gap_padded[:-2, 1:-1])
    east_edge = 0.5 * (centre + gap_padded[1:-1, 2:])
    west_edge = 0.5 * (centre + gap_padded[1:-1, :-2])
    return (north_edge, south_edge, east_edge, west_edge)


def diagonal_of(edge_set, vent_term):
    return edge_set[0] + edge_set[1] + edge_set[2] + edge_set[3] + vent_term


def apply_operator(padded, edge_set, diagonal):
    north_edge, south_edge, east_edge, west_edge = edge_set
    centre = padded[:, :, 1:-1, 1:-1]
    beside_all = (
        north_edge * padded[:, :, 2:, 1:-1]
        + south_edge * padded[:, :, :-2, 1:-1]
        + east_edge * padded[:, :, 1:-1, 2:]
        + west_edge * padded[:, :, 1:-1, :-2]
    )
    turned = jnp.stack([-centre[:, 1], centre[:, 0]], axis=1)
    return diagonal * centre - beside_all + squeeze_number * turned


INTERPRET = False


def sweep_kernel(resid_ref, north_ref, south_ref, east_ref, west_ref, diag_ref, real_ref, scale_ref, out_ref):
    pairs, _, rows, lanes = out_ref.shape
    out_ref[...] = jnp.zeros(out_ref.shape, jnp.float32)

    def sweep(sweep_index, carry):
        for pair_index in range(pairs):
            centre_real = out_ref[pair_index, 0]
            centre_imag = out_ref[pair_index, 1]
            defects = []
            for part, (centre, turned) in enumerate(((centre_real, -centre_imag), (centre_imag, centre_real))):
                beside = (
                    north_ref[...] * pltpu.roll(centre, rows - 1, 0)
                    + south_ref[...] * pltpu.roll(centre, 1, 0)
                    + east_ref[...] * pltpu.roll(centre, lanes - 1, 1)
                    + west_ref[...] * pltpu.roll(centre, 1, 1)
                )
                applied = diag_ref[...] * centre - beside + squeeze_number * turned
                defects.append(resid_ref[pair_index, part] - applied)
            real_diag = real_ref[...]
            step_scale = scale_ref[...]
            update_real = real_diag * defects[0] + squeeze_number * defects[1]
            update_imag = real_diag * defects[1] - squeeze_number * defects[0]
            out_ref[pair_index, 0] = centre_real + step_scale * update_real
            out_ref[pair_index, 1] = centre_imag + step_scale * update_imag
        return carry

    lax.fori_loop(0, SWEEPS, sweep, 0)


def local_solve(residual, edge_set, diagonal, inside):
    real_diag = jnp.where(inside > 0, diagonal, 1.0)
    step_scale = relaxation * inside / (real_diag * real_diag + squeeze_number * squeeze_number)
    rows, cols = diagonal.shape
    lanes = -(-cols // 128) * 128
    row_ids = jnp.arange(rows)[:, None]
    col_ids = jnp.arange(cols)[None, :]
    north_edge, south_edge, east_edge, west_edge = edge_set
    fields = [
        north_edge * (row_ids < rows - 1),
        south_edge * (row_ids > 0),
        east_edge * (col_ids < cols - 1),
        west_edge * (col_ids > 0),
        diagonal,
        real_diag,
        step_scale,
    ]
    widen = lambda field: jnp.pad(field, [(0, 0)] * (field.ndim - 1) + [(0, lanes - cols)])
    vmem = pl.BlockSpec(memory_space=pltpu.VMEM)
    result = pl.pallas_call(
        sweep_kernel,
        out_shape=jax.ShapeDtypeStruct(residual.shape[:2] + (rows, lanes), jnp.float32),
        in_specs=[vmem] * 8,
        out_specs=vmem,
        interpret=INTERPRET,
    )(widen(residual), *[widen(field.astype(jnp.float32)) for field in fields])
    return result[..., :cols]


def complex_scale(alpha_real, alpha_imag, vectors):
    return jnp.stack(
        [
            alpha_real * vectors[..., 0] - alpha_imag * vectors[..., 1],
            alpha_real * vectors[..., 1] + alpha_imag * vectors[..., 0],
        ],
        axis=-1,
    )


def plate_columns(width, tile_cols):
    first_col = lax.axis_index("gy") * tile_cols - width
    col_ids = first_col + jnp.arange(tile_cols + 2 * width, dtype=jnp.int32)
    return ((col_ids >= 0) & (col_ids < tile_cols * lax.axis_size("gy"))).astype(jnp.float32)


def body(forcing, gap_cubed, hole_mask, coarse_bases, basis_counts):
    mode_count = forcing.shape[0]
    tile_rows, tile_cols = gap_cubed.shape
    basis_total = coarse_bases.shape[0]
    deep_width = MARGIN + 1
    wide_rows = tile_rows + 2 * MARGIN
    wide_cols = tile_cols + 2 * MARGIN
    vent_term = vent_gain * hole_mask.astype(jnp.float32) * gap_cubed
    start_stack = jnp.concatenate(
        [gap_cubed[None], vent_term[None], forcing.reshape(2 * mode_count, tile_rows, tile_cols)],
        axis=0,
    )
    grown_stack = padded_2(start_stack, (("gx", 1), ("gy", 2)), deep_width)
    grown_stack = grown_stack * plate_columns(deep_width, tile_cols)
    gap_deep = grown_stack[0]
    vent_wide = grown_stack[1, 1:-1, 1:-1]
    force_wide = grown_stack[2:, 1:-1, 1:-1].reshape(mode_count, 2, wide_rows, wide_cols)
    inside = jnp.broadcast_to(plate_columns(MARGIN, tile_cols)[None, :], (wide_rows, wide_cols))
    wide_edges = edge_terms(gap_deep)
    wide_diag = diagonal_of(wide_edges, vent_wide)
    owned_edges = edge_terms(gap_deep[MARGIN:-MARGIN, MARGIN:-MARGIN])
    owned_diag = diagonal_of(owned_edges, vent_term)
    unit_mask = plate_columns(1, tile_cols)
    active = (jnp.arange(basis_total, dtype=jnp.int32) < basis_counts[0, 0]).astype(jnp.float32)
    base_field = coarse_bases * active[:, None, None]
    flat_bases = base_field.reshape(basis_total, tile_rows * tile_cols)

    def restrict(pressure):
        flat_field = pressure.reshape(2 * mode_count, tile_rows * tile_cols)
        product = lax.dot_general(
            flat_bases,
            flat_field,
            (((1,), (1,)), ((), ())),
            precision=highest,
            preferred_element_type=jnp.float32,
        )
        return product.reshape(basis_total, mode_count, 2)

    def prolong(coarse):
        product = lax.dot_general(
            coarse.reshape(basis_total, 2 * mode_count),
            flat_bases,
            (((0,), (0,)), ((), ())),
            precision=highest,
            preferred_element_type=jnp.float32,
        )
        return product.reshape(mode_count, 2, tile_rows, tile_cols)

    def pair(left, right):
        return lax.dot_general(
            left, right, (((1,), (1,)), ((), ())), precision=highest, preferred_element_type=jnp.float32
        )

    gx_count = lax.axis_size("gx")
    gy_count = lax.axis_size("gy")
    gy_index = lax.axis_index("gy")
    north_edge, south_edge, east_edge, west_edge = owned_edges
    from_next_x = lax.ppermute(base_field[:, 0, :], "gx", [((i + 1) % gx_count, i) for i in range(gx_count)])
    from_prev_x = lax.ppermute(base_field[:, -1, :], "gx", [(i, (i + 1) % gx_count) for i in range(gx_count)])
    from_next_y = lax.ppermute(base_field[:, :, 0], "gy", [((i + 1) % gy_count, i) for i in range(gy_count)])
    from_prev_y = lax.ppermute(base_field[:, :, -1], "gy", [(i, (i + 1) % gy_count) for i in range(gy_count)])
    has_next_y = (gy_index < gy_count - 1).astype(jnp.float32)
    has_prev_y = (gy_index > 0).astype(jnp.float32)
    base_padded = jnp.pad(base_field, ((0, 0), (1, 1), (1, 1)))
    base_image = owned_diag * base_field - (
        north_edge * base_padded[:, 2:, 1:-1]
        + south_edge * base_padded[:, :-2, 1:-1]
        + east_edge * base_padded[:, 1:-1, 2:]
        + west_edge * base_padded[:, 1:-1, :-2]
    )
    self_block = pair(flat_bases, base_image.reshape(basis_total, tile_rows * tile_cols))
    gram_block = pair(flat_bases, flat_bases)
    next_x_block = -pair(base_field[:, -1, :] * north_edge[-1], from_next_x)
    prev_x_block = -pair(base_field[:, 0, :] * south_edge[0], from_prev_x)
    next_y_block = -pair(base_field[:, :, -1] * east_edge[:, -1], from_next_y) * has_next_y
    prev_y_block = -pair(base_field[:, :, 0] * west_edge[:, 0], from_prev_y) * has_prev_y
    block_set = jnp.stack(
        [self_block.T, next_x_block.T, prev_x_block.T, next_y_block.T, prev_y_block.T, squeeze_number * gram_block.T]
    )
    tile_total = gx_count * gy_count
    gathered_blocks = lax.all_gather(block_set.reshape(1, -1), ("gx", "gy"), axis=0, tiled=True)
    all_blocks = lax.dot_general(
        gathered_blocks,
        jnp.eye(tile_total, dtype=jnp.float32),
        (((0,), (0,)), ((), ())),
        precision=highest,
        preferred_element_type=jnp.float32,
    ).reshape(block_set.shape + (tile_total,))

    tile_ids = jnp.arange(tile_total)
    movers = [
        (tile_ids[:, None] == (tile_ids[None, :] + offset) % tile_total).astype(jnp.float32)
        for offset in (gy_count, -gy_count, 1, -1)
    ]

    def coarse_image(search):
        halves = search.reshape(mode_count, 2, basis_total, tile_total)
        turned = jnp.stack([-halves[:, 1], halves[:, 0]], axis=1).reshape(search.shape)
        flat = search.reshape(-1, tile_total)
        moved = [
            lax.dot_general(
                flat, mover, (((1,), (0,)), ((), ())), precision=highest, preferred_element_type=jnp.float32
            ).reshape(search.shape)
            for mover in movers
        ]
        shifted = (search, *moved, turned)
        total = None
        for block, vectors in zip(all_blocks, shifted):
            term = jnp.sum(block[None, :, :, :] * vectors[:, :, None, :], axis=1)
            total = term if total is None else total + term
        return total

    gx_index = lax.axis_index("gx")
    tile_index = gx_index * gy_count + gy_index
    solution = jnp.zeros_like(forcing)
    residual_wide = force_wide
    for outer_step in range(ITERS):
        if outer_step > 0:
            solution_deep = padded_2(solution, (("gx", 2), ("gy", 3)), deep_width) * plate_columns(deep_width, tile_cols)
            residual_wide = force_wide - apply_operator(solution_deep, wide_edges, wide_diag)
            residual_wide = residual_wide * plate_columns(MARGIN, tile_cols)
        residual = residual_wide[:, :, MARGIN:-MARGIN, MARGIN:-MARGIN]
        local_part = local_solve(residual_wide, wide_edges, wide_diag, inside)[
            :, :, MARGIN:-MARGIN, MARGIN:-MARGIN
        ]
        gathered = tree_gather(restrict(residual).reshape(-1), ("gy", "gx"))
        search = gathered.reshape(tile_total, basis_total, 2 * mode_count).transpose(2, 1, 0)
        coarse = jnp.zeros_like(search)
        for coarse_step in range(CSTEPS):
            images = coarse_image(search)
            image_halves = images.reshape(mode_count, 2, basis_total, tile_total)
            search_halves = search.reshape(mode_count, 2, basis_total, tile_total)
            num_real = jnp.sum(
                image_halves[:, 0] * search_halves[:, 0] + image_halves[:, 1] * search_halves[:, 1],
                axis=(1, 2),
            )
            num_imag = jnp.sum(
                image_halves[:, 0] * search_halves[:, 1] - image_halves[:, 1] * search_halves[:, 0],
                axis=(1, 2),
            )
            squares = jnp.sum(image_halves * image_halves, axis=(1, 2, 3))
            denominator = squares + guard_value
            alpha_real = (num_real / denominator)[:, None, None]
            alpha_imag = (num_imag / denominator)[:, None, None]
            coarse_halves = coarse.reshape(search_halves.shape)
            coarse = jnp.stack(
                [
                    coarse_halves[:, 0] + alpha_real * search_halves[:, 0] - alpha_imag * search_halves[:, 1],
                    coarse_halves[:, 1] + alpha_real * search_halves[:, 1] + alpha_imag * search_halves[:, 0],
                ],
                axis=1,
            ).reshape(search.shape)
            search = jnp.stack(
                [
                    search_halves[:, 0] - (alpha_real * image_halves[:, 0] - alpha_imag * image_halves[:, 1]),
                    search_halves[:, 1] - (alpha_real * image_halves[:, 1] + alpha_imag * image_halves[:, 0]),
                ],
                axis=1,
            ).reshape(search.shape)
        own_coarse = lax.dynamic_index_in_dim(coarse, tile_index, axis=2, keepdims=False).T
        solution = solution + local_part + prolong(own_coarse)
    return solution


def solution(mesh):
    placed = (
        P(None, None, "gx", "gy"),
        P("gx", "gy"),
        P("gx", "gy"),
        P(None, "gx", "gy"),
        P("gx", "gy"),
    )
    return jax.shard_map(
        body, mesh=mesh, in_specs=placed, out_specs=P(None, None, "gx", "gy"), check_vma=False
    )
```
